256 devices in a mesh: row: 8 (over y_lo, x), col: 16 (over z, core), layer: 2 (over y_hi).
Axes of the slice: x: 4, y: 4 (y_hi: 2, y_lo: 2; y = y_hi * 2 + y_lo), z: 8, core: 2. Of those that a mesh axis runs over, the one named last changes fastest.
Arguments:
- basis_left: bfloat16 [32768, 32, 128], P(('row', 'col', 'layer')), may hold values from -6 to 6
- basis_right: bfloat16 [32768, 32, 128], P(('row', 'col', 'layer')), may hold values from -6 to 6
- grid_weight: float32 [32768, 128], P(('row', 'col', 'layer')), may hold values from -0.3 to 0.3
- task_owner: int32 [32768, 1], P(('row', 'col', 'layer')), may hold values from 0 to 127; in each aligned block of 128 rows (0 to 127, 128 to 255, ...) at most 2 rows name the same one
- task_block: int32 [32768], P(('row', 'col', 'layer')), may hold values from 0 to 511
- core_matrix: float32 [8192, 8192], P('row', 'col'), may hold values from -6 to 6
- block_mask: int32 [256, 256], P('row', 'col'), may hold values 0 or 1
Outputs:
- ks_matrix: float32 [8192, 8192], P('row', ('col', 'layer'))
- density: float32 [8192, 8192], P('row', ('col', 'layer'))
The draws below stay inside these ranges and needn't reach their ends.
Inputs may be any that keep to these rules, and one draw needn't show every extreme that they name: `task_owner`: in the tasks of one device no owner is named more than 2 times, a bound that some block reaches.
All inputs are finite; a program needn't handle non-finite values. No bound on the sum of `block_mask` on one device may be relied on, other than what follows from the above.
Results may differ from the reference program's by a relative error of at most 0.0053.
Values may be sent and summed in bfloat16 or wider, within the bound.
No kernel may reach another device: no remote copies, remote signals or barrier semaphores. Data moves between devices by JAX's collectives and lax.ppermute only.
A program may use at most 128 MiB of HBM per device.

```python
import math
import jax
import jax.numpy as jnp
import numpy as np
from jax import lax

BS = 32
GRID = 128
NBLK = 256
TASK_DEV = 128
OWNERS = 128
CAP = 2
MAT = 8192
LBLK = 512
TASKS = 32768
N_ROW = 8
N_COL = 16
DEVICES = 256


def place_ends(result, own_key, least, top_value):
    dims = result.shape
    index_at = [jax.random.randint(jax.random.fold_in(own_key, axis), (), 0, dims[axis]) for axis in range(len(dims))]
    result = result.at[tuple(index_at)].set(least)
    longest = dims.index(max(dims))
    index_at[longest] = (index_at[longest] + 1) % dims[longest]
    return result.at[tuple(index_at)].set(top_value)


def steps_of(own_key, dims, split, low, high):
    level = 1.0
    for dim, parts in split:
        steps = jax.random.uniform(jax.random.fold_in(jax.random.fold_in(own_key, 6), dim), (parts,), jnp.float32, low / len(split), high / len(split))
        level = level * jnp.repeat(jnp.exp(steps), dims[dim] // parts).reshape((-1,) + (1,) * (len(dims) - 1 - dim))
    return level


def assign_block(key, own, number, rows, amount, top, most, slope):
    ranking = jax.random.permutation(key, amount)
    heavy_load, ordinary = portions_of(amount, rows * top, most, slope, True), portions_of(amount, rows * top, most, slope, False)
    places = jnp.arange(amount)

    def named(lengths, rotation):
        used = int((lengths > 0).sum())
        fixed = max(1, used // 4)
        shifted = fixed + (places - fixed + rotation * (used - fixed)) % max(1, amount - fixed)
        return jnp.zeros((amount,), jnp.int32).at[ranking[jnp.where(places < fixed, places, shifted)]].set(jnp.asarray(lengths, jnp.int32))

    lengths = jnp.where(number % 4 == 0, named(heavy_load, number // 4), named(ordinary, number - number // 4 - 1))
    mixed = jax.random.permutation(jax.random.fold_in(own, 3), amount)
    source_of, receiver = mixed[0:amount // 2 * 2:2], mixed[1:amount // 2 * 2:2]
    room = jnp.minimum(lengths[source_of] - 1, most - lengths[receiver]) // 2
    room = jnp.where((source_of == ranking[0]) | (receiver == ranking[0]) | (lengths[receiver] == 0), 0, jnp.maximum(room, 0))
    shifted = jax.random.randint(jax.random.fold_in(own, 4), (amount // 2,), 0, 1 << 20) % (room + 1)
    lengths = lengths.at[source_of].add(-shifted).at[receiver].add(shifted)
    members = jnp.searchsorted(jnp.cumsum(lengths), jnp.arange(rows * top), side="right").astype(jnp.int32)
    listing = members.reshape(top, rows).T
    listing = listing[jax.random.permutation(jax.random.fold_in(own, 1), rows)]
    rotation = jax.random.randint(jax.random.fold_in(own, 2), (rows, 1), 0, top)
    return jnp.take_along_axis(listing, (jnp.arange(top)[None, :] + rotation) % top, axis=1)


def portions_of(count, total, most, lean, full):
    portions = [(1 << 20) // math.isqrt(grade ** lean) + 1 for grade in range(1, count + 1)]
    largest = most if full else min(most, max(-(-total // count), total * portions[0] // sum(portions)))
    least = 1 if total - largest >= count - 1 else 0
    given, surplus = [largest] + [least] * (count - 1), total - largest - least * (count - 1)
    while surplus > 0:
        movable = [i for i in range(1, count) if given[i] < largest] or [i for i in range(1, count) if given[i] < most]
        mass, remaining = sum([portions[i] for i in movable]), surplus
        for i in movable:
            extra = min(most - given[i], max(1, remaining * portions[i] // mass), surplus)
            given[i] = given[i] + extra
            surplus = surplus - extra
    return np.array(given)


def scatter_about(own_key, extent, width, most, split=(), kind=jnp.bfloat16):
    entries = jax.random.normal(own_key, extent, jnp.float32) * width
    if len(split) > 0:
        entries = steps_of(own_key, extent, split, -0.22, 0.18) * entries
    return jnp.clip(entries, min=-most, max=most).astype(kind)


def setup_inputs(seed: int = 0) -> dict:
    streams_of = jax.random.split(jax.random.key(seed), 8)
    basis_left = scatter_about(streams_of[0], (TASKS, BS, GRID), 1.0, 6.0, ((0, 256),))
    basis_right = scatter_about(streams_of[1], (TASKS, BS, GRID), 1.0, 6.0, ((0, 256),))
    grid_weight = scatter_about(streams_of[2], (TASKS, GRID), 0.05, 0.3, ((0, 256),), jnp.float32)
    task_owner_keys = jax.random.split(jax.random.fold_in(streams_of[3], 1), TASKS // TASK_DEV)
    task_owner_turns = jax.random.permutation(jax.random.fold_in(streams_of[3], 3), TASKS // TASK_DEV)
    task_owner = jax.vmap(lambda own, number: assign_block(jax.random.fold_in(streams_of[3], 2), own, number, TASK_DEV, OWNERS, 1, CAP, 2))(task_owner_keys, task_owner_turns).reshape((TASKS, 1))
    task_block = place_ends(jax.random.randint(streams_of[4], (TASKS,), 0, LBLK), jax.random.fold_in(streams_of[4], 1), 0, LBLK - 1).astype(jnp.int32)
    core_matrix = scatter_about(streams_of[5], (MAT, MAT), 0.6, 6.0, ((0, 8), (1, 16)), jnp.float32)
    block_mask = place_ends((jax.random.randint(streams_of[6], (NBLK, NBLK), 0, 4) < 1).astype(jnp.int32), jax.random.fold_in(streams_of[6], 1), 0, 1)
    return {"basis_left": basis_left, "basis_right": basis_right, "grid_weight": grid_weight, "task_owner": task_owner, "task_block": task_block, "core_matrix": core_matrix, "block_mask": block_mask}


COUPLING = 2.5

def reference(basis_left, basis_right, grid_weight, task_owner, task_block, core_matrix, block_mask):
    matrix_order = NBLK * BS
    block_rows = NBLK // N_ROW
    block_cols = NBLK // N_COL
    owner_ids = task_owner[:, 0]
    row_ids = owner_ids // N_COL * block_rows + task_block // block_cols
    col_ids = owner_ids % N_COL * block_cols + task_block % block_cols
    flat_ids = (row_ids * NBLK + col_ids).astype(jnp.int32)

    def add_device(accum, inputs):
        left_vals, right_vals, weights, indices = inputs
        weighted = (left_vals.astype(jnp.float32) * weights[:, None, :]).astype(jnp.bfloat16)
        blocks = jnp.einsum('tag,tbg->tab', weighted.astype(jnp.float32), right_vals.astype(jnp.float32))
        return (accum.at[indices].add(blocks.reshape(-1, BS * BS)), None)
    accum, _unused = lax.scan(add_device, jnp.zeros((NBLK * NBLK, BS * BS), jnp.float32), (basis_left.reshape(DEVICES, TASK_DEV, BS, GRID), basis_right.reshape(DEVICES, TASK_DEV, BS, GRID), grid_weight.reshape(DEVICES, TASK_DEV, GRID), flat_ids.reshape(DEVICES, TASK_DEV)))
    grid_terms = accum.reshape(NBLK, NBLK, BS, BS).transpose(0, 2, 1, 3).reshape(matrix_order, matrix_order)
    ks_matrix = core_matrix + grid_terms
    pattern_blocks = (block_mask != 0) | jnp.eye(NBLK, dtype=bool)
    pattern = jnp.repeat(jnp.repeat(pattern_blocks.astype(jnp.float32), BS, 0), BS, 1)
    identity = jnp.eye(matrix_order, dtype=jnp.float32)
    coupling_scale = COUPLING / math.sqrt(matrix_order)
    initial = (pattern * (0.5 * identity - coupling_scale * ks_matrix)).astype(jnp.bfloat16)
    square = pattern * jnp.dot(initial, initial, preferred_element_type=jnp.float32)
    cube_term = pattern * jnp.dot(square.astype(jnp.bfloat16), initial, preferred_element_type=jnp.float32)
    density = 3.0 * square - 2.0 * cube_term
    return (ks_matrix, density)
```

```python
import functools
import math

import jax
import jax.numpy as jnp
from jax import lax
from jax.experimental import pallas as pl
from jax.experimental.pallas import tpu as pltpu
from jax.sharding import Mesh
from jax.sharding import PartitionSpec as P

BS = 32
NBLK = 256
COUPLING = 2.5
AXES = ("ylo", "x", "z", "core", "yhi")
SWAP = [(0, 1), (1, 0)]


def lanes_group(shape):
    return lax.broadcasted_iota(jnp.int32, shape, 1) // BS


def pick(pieces, group):
    out = pieces[0]
    for k in range(1, 4):
        out = jnp.where(group == k, pieces[k], out)
    return out


def contribute_kernel(pos_ref, left_ref, right_ref, weight_ref, out_ref):
    out_ref[...] = jnp.zeros_like(out_ref)
    group = lanes_group((8, 128))

    def body(g, carry):
        base = pl.multiple_of(g * 8, 8)
        w = weight_ref[pl.ds(base, 8), :]
        left = left_ref[pl.ds(base, 8)].astype(jnp.float32) * w[:, None, :]
        left = left.astype(jnp.bfloat16).reshape(256, 128)
        right = right_ref[pl.ds(base, 8)].reshape(256, 128)
        for half in range(2):
            c = lax.dot_general(
                left[half * 128 : half * 128 + 128],
                right[half * 128 : half * 128 + 128],
                (((1,), (1,)), ((), ())),
                preferred_element_type=jnp.float32,
            )
            for t in range(4):
                rows = [c[32 * t + 8 * k : 32 * t + 8 * k + 8, :] for k in range(4)]
                rows = [
                    rows[k] if k == t else pltpu.roll(rows[k], (32 * (k - t)) % 128, 1)
                    for k in range(4)
                ]
                out_ref[pos_ref[base + half * 4 + t]] = pick(rows, group).astype(jnp.bfloat16)
        return carry

    lax.fori_loop(0, 16, body, 0)


def accumulate(acc_ref, label_ref, slot_ref):
    acc_ref[...] = jnp.zeros_like(acc_ref)

    def body(s, carry):
        for u in range(8):
            n = label_ref[s * 8 + u]
            acc_ref[n] = acc_ref[n] + slot_ref[s * 8 + u].astype(jnp.float32)
        return carry

    lax.fori_loop(0, slot_ref.shape[0] // 8, body, 0)


def collect_kernel(label_ref, slot_ref, acc_ref):
    accumulate(acc_ref, label_ref, slot_ref)


def assemble_kernel(
    place_ref, mask_ref, label_ref, slot_ref, first_ref, core_ref,
    ks_ref, own_ref, panel_ref, pattern_ref, second_ref, *, scale,
):
    accumulate(second_ref, label_ref, slot_ref)
    row, col, half_own = place_ref[0], place_ref[1], place_ref[2]
    group = lanes_group((8, 128))
    sub = lax.broadcasted_iota(jnp.int32, (8, 128), 0)
    lane = lax.broadcasted_iota(jnp.int32, (8, 128), 1)

    def body(i, carry):
        r0 = pl.multiple_of(i * 32, 32)
        quarter = i // 8
        q0 = pl.multiple_of((i % 8) * 32, 32)
        block_row = row * 32 + i
        for jt in range(4):
            half = jt // 2
            blocks, marks = [], []
            for j in range(4):
                n = i * 16 + jt * 4 + j
                blocks.append(first_ref[n] + second_ref[n])
                on = (mask_ref[n] != 0) | (block_row == col * 16 + jt * 4 + j)
                marks.append(jnp.full((8, 128), on.astype(jnp.float32)))
            pat = pick(marks, group)
            ks_rows, x_rows = [], []
            for t in range(4):
                turned = [
                    blocks[j] if j == t else pltpu.roll(blocks[j], (32 * (j - t)) % 128, 1)
                    for j in range(4)
                ]
                ks = core_ref[pl.ds(r0 + 8 * t, 8), jt * 128 : jt * 128 + 128] + pick(turned, group)
                identity = (
                    row * 1024 + r0 + 8 * t + sub == col * 512 + jt * 128 + lane
                ).astype(jnp.float32)
                ks_rows.append(ks)
                x_rows.append(pat * (0.5 * identity - scale * ks))
            x = jnp.concatenate(x_rows, axis=0).astype(jnp.bfloat16)
            inner = (jt % 2) * 128
            other = half != half_own
            at = pl.multiple_of(other.astype(jnp.int32) * 256 + inner, 128)
            panel_ref[quarter, pl.ds(q0, 32), pl.ds(at, 128)] = x

            @pl.when(jnp.logical_not(other))
            def _():
                ks_ref[pl.ds(r0, 32), inner : inner + 128] = jnp.concatenate(ks_rows, axis=0)
                own_ref[pl.ds(r0, 32), inner : inner + 128] = x
                pattern_ref[pl.ds(r0, 32), inner : inner + 128] = jnp.concatenate(
                    [pat] * 4, axis=0
                ).astype(jnp.bfloat16)

        return carry

    lax.fori_loop(0, 32, body, 0)


VMEM = pl.BlockSpec(memory_space=pltpu.VMEM)
SMEM = pl.BlockSpec(memory_space=pltpu.SMEM)


def contribute(pos, left, right, weight):
    tasks = left.shape[0]
    return pl.pallas_call(
        contribute_kernel,
        out_shape=jax.ShapeDtypeStruct((2 * tasks, 8, 128), jnp.bfloat16),
        in_specs=[SMEM, VMEM, VMEM, VMEM],
        out_specs=VMEM,
        name="contribute",
    )(pos, left, right, weight)


def collect(labels, slots):
    return pl.pallas_call(
        collect_kernel,
        out_shape=jax.ShapeDtypeStruct((520, 8, 128), jnp.float32),
        in_specs=[SMEM, VMEM],
        out_specs=VMEM,
        cost_estimate=pl.CostEstimate(flops=1 << 20, bytes_accessed=1 << 23, transcendentals=0),
        name="collect",
    )(labels, slots)


def assemble(place, mask, labels, slots, first, core):
    return pl.pallas_call(
        functools.partial(assemble_kernel, scale=COUPLING / math.sqrt(NBLK * BS)),
        out_shape=(
            jax.ShapeDtypeStruct((1024, 256), jnp.float32),
            jax.ShapeDtypeStruct((1024, 256), jnp.bfloat16),
            jax.ShapeDtypeStruct((4, 256, 512), jnp.bfloat16),
            jax.ShapeDtypeStruct((1024, 256), jnp.bfloat16),
        ),
        in_specs=[SMEM, SMEM, SMEM, VMEM, VMEM, VMEM],
        out_specs=(VMEM, VMEM, VMEM, VMEM),
        scratch_shapes=[pltpu.VMEM((520, 8, 128), jnp.float32)],
        name="assemble",
    )(place, mask, labels, slots, first, core)


def ring_of(n, step):
    return [(i, (i + step) % n) for i in range(n)]


def gather_z(own):
    pieces = [own] + [None] * 7
    up = down = own
    for s in range(1, 4):
        up = lax.ppermute(up, "z", ring_of(8, 1))
        down = lax.ppermute(down, "z", ring_of(8, -1))
        pieces[8 - s], pieces[s] = up, down
    top = lax.ppermute(up[:512], "z", ring_of(8, 1))
    bottom = lax.ppermute(down[512:], "z", ring_of(8, -1))
    pieces[4] = jnp.concatenate([top, bottom], axis=0)
    return jnp.concatenate(pieces, axis=1)


def gather_rows(unit, ylo, x, z):
    fwd, bwd = ring_of(4, 1), ring_of(4, -1)
    near = lax.ppermute(unit, "ylo", SWAP)
    a1 = lax.ppermute(unit, "x", fwd)
    a3 = lax.ppermute(unit, "x", bwd)
    b1 = lax.ppermute(near, "x", fwd)
    b3 = lax.ppermute(near, "x", bwd)
    a2 = lax.ppermute(a1, "x", fwd)
    b2 = lax.ppermute(b3, "x", bwd)
    out = jnp.zeros((8,) + unit.shape, unit.dtype)
    for flip, dx, piece in (
        (0, 0, unit), (1, 0, near), (0, 3, a1), (0, 1, a3),
        (1, 3, b1), (1, 1, b3), (0, 2, a2), (1, 2, b2),
    ):
        source = (ylo ^ flip) * 4 + (x + dx) % 4
        out = lax.dynamic_update_index_in_dim(out, piece, (source - z) % 8, 0)
    return out.reshape(8 * unit.shape[0], unit.shape[1])


def product(a, b):
    far = jnp.dot(a, b[:, 512:], preferred_element_type=jnp.float32).astype(jnp.bfloat16)
    far = lax.ppermute(far, "core", SWAP)
    near = jnp.dot(a, b[:, :512], preferred_element_type=jnp.float32)
    part = near + far.astype(jnp.float32)
    away = lax.ppermute(part[:, 256:].astype(jnp.bfloat16), "yhi", SWAP)
    return part[:, :256] + away.astype(jnp.float32)


def local(basis_left, basis_right, grid_weight, task_owner, task_block, core_matrix, block_mask):
    ylo, x, z, core, yhi = (lax.axis_index(a) for a in AXES)
    row, col = ylo * 4 + x, z * 2 + core
    owner = row * 16 + col
    tasks = basis_left.shape[0]

    target = task_owner[:, 0]
    tags = lax.all_gather(target * 512 + task_block, AXES, axis=0, tiled=False)
    order = jnp.arange(tasks, dtype=jnp.int32)
    earlier = (target[:, None] == target[None, :]) & (order[None, :] < order[:, None])
    pos = target * 2 + jnp.sum(earlier.astype(jnp.int32), axis=1)

    outgoing = contribute(pos, basis_left, basis_right, grid_weight)
    arrived = lax.all_to_all(
        outgoing.reshape(tasks, 2, 8, 128), AXES[:4], split_axis=0, concat_axis=0, tiled=True
    ).reshape(2 * tasks, 8, 128)

    mine = tags // 512 == owner
    first = jnp.min(jnp.where(mine, order[None, :], tasks), axis=1, keepdims=True)
    last = jnp.max(jnp.where(mine, order[None, :], -1), axis=1, keepdims=True)
    block = tags % 512
    label0 = jnp.sum(jnp.where(order[None, :] == first, block, 0), axis=1)
    label1 = jnp.sum(jnp.where(order[None, :] == last, block, 0), axis=1)
    label0 = jnp.where(last[:, 0] >= 0, label0, 512)
    label1 = jnp.where(last[:, 0] > first[:, 0], label1, 512)
    labels = jnp.stack([label0, label1], axis=1).reshape(tasks, 2, 2)
    labels_own = lax.dynamic_index_in_dim(labels, yhi, 1, keepdims=False).reshape(-1)
    labels_far = lax.dynamic_index_in_dim(labels, 1 - yhi, 1, keepdims=False).reshape(-1)

    arrived_far = lax.ppermute(arrived, "yhi", SWAP)
    collected = collect(labels_own, arrived)
    place = jnp.stack([row, col, yhi]).astype(jnp.int32)
    ks_out, own, panel, pattern = assemble(
        place, block_mask.reshape(-1), labels_far, arrived_far, collected, core_matrix
    )

    keep = lax.dynamic_index_in_dim(panel, 2 * core + yhi, 0, keepdims=False)
    give = lax.dynamic_index_in_dim(panel, 2 * (1 - core) + yhi, 0, keepdims=False)
    unit = jnp.concatenate([keep, lax.ppermute(give, "core", SWAP)], axis=1)
    b = gather_rows(unit, ylo, x, z)
    pattern = pattern.astype(jnp.float32)
    square = pattern * product(gather_z(own), b)
    cube_term = pattern * product(gather_z(square.astype(jnp.bfloat16)), b)
    density = 3.0 * square - 2.0 * cube_term
    return (ks_out, density)


def solution(mesh):
    fine = Mesh(mesh.devices.reshape(2, 4, 8, 2, 2), AXES)
    spread = AXES
    rows, cols = ("ylo", "x"), ("z", "core")
    placed = (
        P(spread, None, None),
        P(spread, None, None),
        P(spread, None),
        P(spread, None),
        P(spread),
        P(rows, cols),
        P(rows, cols),
    )
    return jax.shard_map(
        local,
        mesh=fine,
        in_specs=placed,
        out_specs=(P(rows, cols + ("yhi",)), P(rows, cols + ("yhi",))),
        check_vma=False,
    )
```

```python
import functools
import math

import jax
import jax.numpy as jnp
from jax import lax
from jax.experimental import pallas as pl
from jax.experimental.pallas import tpu as pltpu
from jax.sharding import Mesh
from jax.sharding import PartitionSpec as P

BS = 32
NBLK = 256
COUPLING = 2.5
AXES = ("ylo", "x", "z", "core", "yhi")
SWAP = [(0, 1), (1, 0)]


def lanes_group(shape):
    return lax.broadcasted_iota(jnp.int32, shape, 1) // BS


def pick(pieces, group):
    out = pieces[0]
    for k in range(1, 4):
        out = jnp.where(group == k, pieces[k], out)
    return out


def contribute_kernel(pos_ref, block_ref, left_ref, right_ref, weight_ref, out_ref):
    out_ref[...] = jnp.full(out_ref.shape, 32.0, out_ref.dtype)
    group = lanes_group((8, 128))
    sub = lax.broadcasted_iota(jnp.int32, (8, 128), 0)
    lane = lax.broadcasted_iota(jnp.int32, (8, 128), 1)

    def body(g, carry):
        base = pl.multiple_of(g * 8, 8)
        w = weight_ref[pl.ds(base, 8), :]
        left = left_ref[pl.ds(base, 8)].astype(jnp.float32) * w[:, None, :]
        left = left.astype(jnp.bfloat16).reshape(256, 128)
        right = right_ref[pl.ds(base, 8)].reshape(256, 128)
        for half in range(2):
            c = lax.dot_general(
                left[half * 128 : half * 128 + 128],
                right[half * 128 : half * 128 + 128],
                (((1,), (1,)), ((), ())),
                preferred_element_type=jnp.float32,
            )
            for t in range(4):
                rows = [c[32 * t + 8 * k : 32 * t + 8 * k + 8, :] for k in range(4)]
                rows = [
                    rows[k] if k == t else pltpu.roll(rows[k], (32 * (k - t)) % 128, 1)
                    for k in range(4)
                ]
                task = base + half * 4 + t
                owner, slot = pos_ref[task] >> 1, pos_ref[task] & 1
                out_ref[owner * 3 + slot] = pick(rows, group).astype(jnp.bfloat16)
                block = block_ref[task]
                high = (block >> 4).astype(jnp.float32)
                low = (block & 15).astype(jnp.float32)
                tag = out_ref[owner * 3 + 2].astype(jnp.float32)
                tag = jnp.where(sub == slot, jnp.where(lane == 0, high, low), tag)
                out_ref[owner * 3 + 2] = tag.astype(jnp.bfloat16)
        return carry

    lax.fori_loop(0, 16, body, 0)


def accumulate(acc_ref, label_ref, slot_ref, stride):
    def body(s, carry):
        for u in range(8):
            n = label_ref[s * 8 + u]
            at = (s * 4 + u // 2) * stride + u % 2
            acc_ref[n] = acc_ref[n] + slot_ref[at].astype(jnp.float32)
        return carry

    lax.fori_loop(0, label_ref.shape[0] // 8, body, 0)


def collect_kernel(label_ref, slot_ref, acc_ref):
    acc_ref[...] = jnp.zeros_like(acc_ref)
    accumulate(acc_ref, label_ref, slot_ref, 3)


def assemble_kernel(
    place_ref, mask_ref, label_ref, slot_ref, first_ref, core_ref,
    ks_ref, own_ref, panel_ref, pattern_ref, acc_ref, *, scale,
):
    acc_ref[...] = first_ref[...]
    accumulate(acc_ref, label_ref, slot_ref, 2)
    row, col, half_own = place_ref[0], place_ref[1], place_ref[2]
    group = lanes_group((8, 128))
    sub = lax.broadcasted_iota(jnp.int32, (8, 128), 0)
    lane = lax.broadcasted_iota(jnp.int32, (8, 128), 1)
    slant = sub - lane

    def body(i, carry):
        r0 = pl.multiple_of(i * 32, 32)
        quarter = i // 8
        q0 = pl.multiple_of((i % 8) * 32, 32)
        for side in range(2):
            half = half_own if side == 0 else 1 - half_own
            for jt in range(2):
                n = i * 16 + half * 8 + jt * 4
                blocks = [acc_ref[n + j] for j in range(4)]
                pat = pick([jnp.full((8, 128), mask_ref[n + j]) for j in range(4)], group)
                c0 = pl.multiple_of(half * 256 + jt * 128, 128)
                gap = col * 512 + c0 - row * 1024 - r0
                ks_rows, x_rows = [], []
                for t in range(4):
                    turned = [
                        blocks[j] if j == t else pltpu.roll(blocks[j], (32 * (j - t)) % 128, 1)
                        for j in range(4)
                    ]
                    ks = core_ref[pl.ds(r0 + 8 * t, 8), pl.ds(c0, 128)] + pick(turned, group)
                    identity = jnp.where(slant == gap - 8 * t, 0.5, 0.0)
                    ks_rows.append(ks)
                    x_rows.append(pat * (identity - scale * ks))
                x = jnp.concatenate(x_rows, axis=0).astype(jnp.bfloat16)
                panel_ref[quarter, pl.ds(q0, 32), side * 256 + jt * 128 : side * 256 + jt * 128 + 128] = x
                if side == 0:
                    at = slice(jt * 128, jt * 128 + 128)
                    ks_ref[pl.ds(r0, 32), at] = jnp.concatenate(ks_rows, axis=0)
                    own_ref[pl.ds(r0, 32), at] = x
                    pattern_ref[pl.ds(r0, 32), at] = jnp.concatenate([pat] * 4, axis=0).astype(
                        jnp.bfloat16
                    )
        return carry

    lax.fori_loop(0, 32, body, 0)


VMEM = pl.BlockSpec(memory_space=pltpu.VMEM)
SMEM = pl.BlockSpec(memory_space=pltpu.SMEM)


def contribute(pos, block, left, right, weight):
    tasks = left.shape[0]
    return pl.pallas_call(
        contribute_kernel,
        out_shape=jax.ShapeDtypeStruct((3 * tasks, 8, 128), jnp.bfloat16),
        in_specs=[SMEM, SMEM, VMEM, VMEM, VMEM],
        out_specs=VMEM,
        name="contribute",
    )(pos, block, left, right, weight)


def collect(labels, slots):
    return pl.pallas_call(
        collect_kernel,
        out_shape=jax.ShapeDtypeStruct((520, 8, 128), jnp.float32),
        in_specs=[SMEM, VMEM],
        out_specs=VMEM,
        cost_estimate=pl.CostEstimate(flops=1 << 20, bytes_accessed=1 << 23, transcendentals=0),
        name="collect",
    )(labels, slots)


def assemble(place, mask, labels, slots, first, core):
    return pl.pallas_call(
        functools.partial(assemble_kernel, scale=COUPLING / math.sqrt(NBLK * BS)),
        out_shape=(
            jax.ShapeDtypeStruct((1024, 256), jnp.float32),
            jax.ShapeDtypeStruct((1024, 256), jnp.bfloat16),
            jax.ShapeDtypeStruct((4, 256, 512), jnp.bfloat16),
            jax.ShapeDtypeStruct((1024, 256), jnp.bfloat16),
        ),
        in_specs=[SMEM, SMEM, SMEM, VMEM, VMEM, VMEM],
        out_specs=(VMEM, VMEM, VMEM, VMEM),
        scratch_shapes=[pltpu.VMEM((520, 8, 128), jnp.float32)],
        name="assemble",
    )(place, mask, labels, slots, first, core)


def ring_of(n, step):
    return [(i, (i + step) % n) for i in range(n)]


def gather_z(own):
    pieces = [own] + [None] * 7
    up = down = own
    for s in range(1, 4):
        up = lax.ppermute(up, "z", ring_of(8, 1))
        down = lax.ppermute(down, "z", ring_of(8, -1))
        pieces[8 - s], pieces[s] = up, down
    top = lax.ppermute(up[:512], "z", ring_of(8, 1))
    bottom = lax.ppermute(down[512:], "z", ring_of(8, -1))
    pieces[4] = jnp.concatenate([top, bottom], axis=0)
    return jnp.concatenate(pieces, axis=1)


def gather_rows(unit, ylo, x, z):
    fwd, bwd = ring_of(4, 1), ring_of(4, -1)
    near = lax.ppermute(unit, "ylo", SWAP)
    a1 = lax.ppermute(unit, "x", fwd)
    a3 = lax.ppermute(unit, "x", bwd)
    b1 = lax.ppermute(near, "x", fwd)
    b3 = lax.ppermute(near, "x", bwd)
    a2 = lax.ppermute(a1, "x", fwd)
    b2 = lax.ppermute(b3, "x", bwd)
    out = jnp.zeros((8,) + unit.shape, unit.dtype)
    for flip, dx, piece in (
        (0, 0, unit), (1, 0, near), (0, 3, a1), (0, 1, a3),
        (1, 3, b1), (1, 1, b3), (0, 2, a2), (1, 2, b2),
    ):
        source = (ylo ^ flip) * 4 + (x + dx) % 4
        out = lax.dynamic_update_index_in_dim(out, piece, (source - z) % 8, 0)
    return out.reshape(8 * unit.shape[0], unit.shape[1])


def product(a, b):
    far = jnp.dot(a, b[:, 512:], preferred_element_type=jnp.float32).astype(jnp.bfloat16)
    far = lax.ppermute(far, "core", SWAP)
    near = jnp.dot(a, b[:, :512], preferred_element_type=jnp.float32)
    part = near + far.astype(jnp.float32)
    away = lax.ppermute(part[:, 256:].astype(jnp.bfloat16), "yhi", SWAP)
    return part[:, :256] + away.astype(jnp.float32)


def local(basis_left, basis_right, grid_weight, task_owner, task_block, core_matrix, block_mask):
    ylo, x, z, core, yhi = (lax.axis_index(a) for a in AXES)
    row, col = ylo * 4 + x, z * 2 + core
    tasks = basis_left.shape[0]

    target = task_owner[:, 0]
    order = jnp.arange(tasks, dtype=jnp.int32)
    earlier = (target[:, None] == target[None, :]) & (order[None, :] < order[:, None])
    pos = target * 2 + jnp.sum(earlier.astype(jnp.int32), axis=1)

    outgoing = contribute(pos, task_block, basis_left, basis_right, grid_weight)
    arrived = lax.all_to_all(
        outgoing.reshape(tasks, 3, 8, 128), AXES[:4], split_axis=0, concat_axis=0, tiled=True
    )
    tag = arrived[:, 2, :2, :2].astype(jnp.float32)
    labels = jnp.minimum(tag[:, :, 0] * 16 + tag[:, :, 1], 512.0).astype(jnp.int32).reshape(-1)
    labels_far = lax.ppermute(labels, "yhi", SWAP)
    arrived_far = lax.ppermute(arrived[:, :2].reshape(2 * tasks, 8, 128), "yhi", SWAP)
    collected = collect(labels, arrived.reshape(3 * tasks, 8, 128))
    block_rows = row * 32 + jnp.arange(32, dtype=jnp.int32)
    block_cols = col * 16 + jnp.arange(16, dtype=jnp.int32)
    mask = (block_mask != 0) | (block_rows[:, None] == block_cols[None, :])
    place = jnp.stack([row, col, yhi]).astype(jnp.int32)
    ks_out, own, panel, pattern = assemble(
        place, mask.astype(jnp.float32).reshape(-1), labels_far, arrived_far, collected, core_matrix
    )

    keep = lax.dynamic_index_in_dim(panel, 2 * core + yhi, 0, keepdims=False)
    give = lax.dynamic_index_in_dim(panel, 2 * (1 - core) + yhi, 0, keepdims=False)
    unit = jnp.concatenate([keep, lax.ppermute(give, "core", SWAP)], axis=1)
    b = gather_rows(unit, ylo, x, z)
    pattern = pattern.astype(jnp.float32)
    square = pattern * product(gather_z(own), b)
    cube_term = pattern * product(gather_z(square.astype(jnp.bfloat16)), b)
    density = 3.0 * square - 2.0 * cube_term
    return (ks_out, density)


def solution(mesh):
    fine = Mesh(mesh.devices.reshape(2, 4, 8, 2, 2), AXES)
    spread = AXES
    rows, cols = ("ylo", "x"), ("z", "core")
    placed = (
        P(spread, None, None),
        P(spread, None, None),
        P(spread, None),
        P(spread, None),
        P(spread),
        P(rows, cols),
        P(rows, cols),
    )
    return jax.shard_map(
        local,
        mesh=fine,
        in_specs=placed,
        out_specs=(P(rows, cols + ("yhi",)), P(rows, cols + ("yhi",))),
        check_vma=False,
    )
```

```python
import functools
import math

import jax
import jax.numpy as jnp
from jax import lax
from jax.experimental import pallas as pl
from jax.experimental.pallas import tpu as pltpu
from jax.sharding import Mesh
from jax.sharding import PartitionSpec as P

BS = 32
NBLK = 256
COUPLING = 2.5
AXES = ("ylo", "x", "z", "core", "yhi")
SWAP = [(0, 1), (1, 0)]


def lanes_group(shape):
    return lax.broadcasted_iota(jnp.int32, shape, 1) // BS


def pick(pieces, group):
    out = pieces[0]
    for k in range(1, 4):
        out = jnp.where(group == k, pieces[k], out)
    return out


def contribute_kernel(pos_ref, block_ref, left_ref, right_ref, weight_ref, out_ref):
    out_ref[...] = jnp.full(out_ref.shape, 32.0, out_ref.dtype)
    group = lanes_group((8, 128))
    sub = lax.broadcasted_iota(jnp.int32, (8, 128), 0)
    lane = lax.broadcasted_iota(jnp.int32, (8, 128), 1)

    def body(g, carry):
        base = pl.multiple_of(g * 8, 8)
        w = weight_ref[pl.ds(base, 8), :]
        left = left_ref[pl.ds(base, 8)].astype(jnp.float32) * w[:, None, :]
        left = left.astype(jnp.bfloat16).reshape(256, 128)
        right = right_ref[pl.ds(base, 8)].reshape(256, 128)
        for half in range(2):
            c = lax.dot_general(
                left[half * 128 : half * 128 + 128],
                right[half * 128 : half * 128 + 128],
                (((1,), (1,)), ((), ())),
                preferred_element_type=jnp.float32,
            )
            for t in range(4):
                rows = [c[32 * t + 8 * k : 32 * t + 8 * k + 8, :] for k in range(4)]
                rows = [
                    rows[k] if k == t else pltpu.roll(rows[k], (32 * (k - t)) % 128, 1)
                    for k in range(4)
                ]
                task = base + half * 4 + t
                owner, slot = pos_ref[task] >> 1, pos_ref[task] & 1
                out_ref[owner * 3 + slot] = pick(rows, group).astype(jnp.bfloat16)
                block = block_ref[task]
                high = (block >> 4).astype(jnp.float32)
                low = (block & 15).astype(jnp.float32)
                tag = out_ref[owner * 3 + 2].astype(jnp.float32)
                tag = jnp.where(sub == slot, jnp.where(lane == 0, high, low), tag)
                out_ref[owner * 3 + 2] = tag.astype(jnp.bfloat16)
        return carry

    lax.fori_loop(0, 16, body, 0)


def accumulate(acc_ref, label_ref, slot_ref, stride):
    def body(s, carry):
        for u in range(8):
            n = label_ref[s * 8 + u]
            at = (s * 4 + u // 2) * stride + u % 2
            acc_ref[n] = acc_ref[n] + slot_ref[at].astype(jnp.float32)
        return carry

    lax.fori_loop(0, label_ref.shape[0] // 8, body, 0)


def collect_kernel(label_ref, slot_ref, acc_ref):
    acc_ref[...] = jnp.zeros_like(acc_ref)
    accumulate(acc_ref, label_ref, slot_ref, 3)


def assemble_kernel(
    place_ref, mask_ref, label_ref, slot_ref, first_ref, core_ref,
    ks_ref, own_ref, panel_ref, pattern_ref, acc_ref, *, scale,
):
    acc_ref[...] = first_ref[...]
    accumulate(acc_ref, label_ref, slot_ref, 2)
    row, col, half_own = place_ref[0], place_ref[1], place_ref[2]
    group = lanes_group((8, 128))
    sub = lax.broadcasted_iota(jnp.int32, (8, 128), 0)
    lane = lax.broadcasted_iota(jnp.int32, (8, 128), 1)
    slant = sub - lane

    def body(i, carry):
        r0 = pl.multiple_of(i * 32, 32)
        quarter = i // 8
        q0 = pl.multiple_of((i % 8) * 32, 32)
        for side in range(2):
            half = half_own if side == 0 else 1 - half_own
            for jt in range(2):
                n = i * 16 + half * 8 + jt * 4
                blocks = [acc_ref[n + j] for j in range(4)]
                pat = pick([jnp.full((8, 128), mask_ref[n + j]) for j in range(4)], group)
                c0 = pl.multiple_of(half * 256 + jt * 128, 128)
                gap = col * 512 + c0 - row * 1024 - r0
                ks_rows, x_rows = [], []
                for t in range(4):
                    turned = [
                        blocks[j] if j == t else pltpu.roll(blocks[j], (32 * (j - t)) % 128, 1)
                        for j in range(4)
                    ]
                    ks = core_ref[pl.ds(r0 + 8 * t, 8), pl.ds(c0, 128)] + pick(turned, group)
                    identity = jnp.where(slant == gap - 8 * t, 0.5, 0.0)
                    ks_rows.append(ks)
                    x_rows.append(pat * (identity - scale * ks))
                x = jnp.concatenate(x_rows, axis=0).astype(jnp.bfloat16)
                panel_ref[quarter, pl.ds(q0, 32), side * 256 + jt * 128 : side * 256 + jt * 128 + 128] = x
                if side == 0:
                    at = slice(jt * 128, jt * 128 + 128)
                    ks_ref[pl.ds(r0, 32), at] = jnp.concatenate(ks_rows, axis=0)
                    own_ref[pl.ds(r0, 32), at] = x
                    pattern_ref[pl.ds(r0, 32), at] = jnp.concatenate([pat] * 4, axis=0).astype(
                        jnp.bfloat16
                    )
        return carry

    lax.fori_loop(0, 32, body, 0)


VMEM = pl.BlockSpec(memory_space=pltpu.VMEM)
SMEM = pl.BlockSpec(memory_space=pltpu.SMEM)


def contribute(pos, block, left, right, weight):
    tasks = left.shape[0]
    return pl.pallas_call(
        contribute_kernel,
        out_shape=jax.ShapeDtypeStruct((3 * tasks, 8, 128), jnp.bfloat16),
        in_specs=[SMEM, SMEM, VMEM, VMEM, VMEM],
        out_specs=VMEM,
        name="contribute",
    )(pos, block, left, right, weight)


def collect(labels, slots):
    return pl.pallas_call(
        collect_kernel,
        out_shape=jax.ShapeDtypeStruct((520, 8, 128), jnp.float32),
        in_specs=[SMEM, VMEM],
        out_specs=VMEM,
        cost_estimate=pl.CostEstimate(flops=1 << 20, bytes_accessed=1 << 23, transcendentals=0),
        name="collect",
    )(labels, slots)


def assemble(place, mask, labels, slots, first, core):
    return pl.pallas_call(
        functools.partial(assemble_kernel, scale=COUPLING / math.sqrt(NBLK * BS)),
        out_shape=(
            jax.ShapeDtypeStruct((1024, 256), jnp.float32),
            jax.ShapeDtypeStruct((1024, 256), jnp.bfloat16),
            jax.ShapeDtypeStruct((4, 256, 512), jnp.bfloat16),
            jax.ShapeDtypeStruct((1024, 256), jnp.bfloat16),
        ),
        in_specs=[SMEM, SMEM, SMEM, VMEM, VMEM, VMEM],
        out_specs=(VMEM, VMEM, VMEM, VMEM),
        scratch_shapes=[pltpu.VMEM((520, 8, 128), jnp.float32)],
        name="assemble",
    )(place, mask, labels, slots, first, core)


def ring_of(n, step):
    return [(i, (i + step) % n) for i in range(n)]


def gather_z(own, first):
    pieces = [own] + [None] * 7
    up = down = own
    for s in range(1, 5):
        if s < 4 or first:
            up = lax.ppermute(up, "z", ring_of(8, 1))
            pieces[8 - s] = up
        if s < 4 or not first:
            down = lax.ppermute(down, "z", ring_of(8, -1))
            pieces[s] = down
    return jnp.concatenate(pieces, axis=1)


def gather_z_whole(own):
    pieces = [own] + [None] * 7
    up = down = own
    for s in range(1, 4):
        up = lax.ppermute(up, "z", ring_of(8, 1))
        down = lax.ppermute(down, "z", ring_of(8, -1))
        pieces[8 - s], pieces[s] = up, down
    middle = (
        lax.ppermute(up[:512], "z", ring_of(8, 1)),
        lax.ppermute(down[512:], "z", ring_of(8, -1)),
    )
    chunks = []
    for m in range(2):
        parts = [None if p is None else p[512 * m : 512 * m + 512] for p in pieces]
        parts[4] = middle[m]
        chunks.append(jnp.concatenate(parts, axis=1))
    return chunks


def gather_rows(unit, ylo, x, z):
    fwd, bwd = ring_of(4, 1), ring_of(4, -1)
    near = lax.ppermute(unit, "ylo", SWAP)
    a1 = lax.ppermute(unit, "x", fwd)
    a3 = lax.ppermute(unit, "x", bwd)
    b1 = lax.ppermute(near, "x", fwd)
    b3 = lax.ppermute(near, "x", bwd)
    a2 = lax.ppermute(a1, "x", fwd)
    b2 = lax.ppermute(b3, "x", bwd)
    out = jnp.zeros((8,) + unit.shape, unit.dtype)
    for flip, dx, piece in (
        (0, 0, unit), (1, 0, near), (0, 3, a1), (0, 1, a3),
        (1, 3, b1), (1, 1, b3), (0, 2, a2), (1, 2, b2),
    ):
        source = (ylo ^ flip) * 4 + (x + dx) % 4
        out = lax.dynamic_update_index_in_dim(out, piece, (source - z) % 8, 0)
    return out.reshape(8 * unit.shape[0], unit.shape[1])


def product(a, b):
    def dot(columns):
        return jnp.dot(a, b[:, columns], preferred_element_type=jnp.float32)

    far = lax.ppermute(dot(slice(512, 1024)).astype(jnp.bfloat16), "core", SWAP)
    away = dot(slice(256, 512)) + far[:, 256:].astype(jnp.float32)
    away = lax.ppermute(away.astype(jnp.bfloat16), "yhi", SWAP)
    return dot(slice(0, 256)) + far[:, :256].astype(jnp.float32) + away.astype(jnp.float32)


def local(basis_left, basis_right, grid_weight, task_owner, task_block, core_matrix, block_mask):
    ylo, x, z, core, yhi = (lax.axis_index(a) for a in AXES)
    row, col = ylo * 4 + x, z * 2 + core
    tasks = basis_left.shape[0]

    target = task_owner[:, 0]
    order = jnp.arange(tasks, dtype=jnp.int32)
    earlier = (target[:, None] == target[None, :]) & (order[None, :] < order[:, None])
    pos = target * 2 + jnp.sum(earlier.astype(jnp.int32), axis=1)

    outgoing = contribute(pos, task_block, basis_left, basis_right, grid_weight)
    arrived = lax.all_to_all(
        outgoing.reshape(tasks, 3, 8, 128), AXES[:4], split_axis=0, concat_axis=0, tiled=True
    )
    tag = arrived[:, 2, :2, :2].astype(jnp.float32)
    labels = jnp.minimum(tag[:, :, 0] * 16 + tag[:, :, 1], 512.0).astype(jnp.int32).reshape(-1)
    labels_far = lax.ppermute(labels, "yhi", SWAP)
    arrived_far = lax.ppermute(arrived[:, :2].reshape(2 * tasks, 8, 128), "yhi", SWAP)
    collected = collect(labels, arrived.reshape(3 * tasks, 8, 128))
    block_rows = row * 32 + jnp.arange(32, dtype=jnp.int32)
    block_cols = col * 16 + jnp.arange(16, dtype=jnp.int32)
    mask = (block_mask != 0) | (block_rows[:, None] == block_cols[None, :])
    place = jnp.stack([row, col, yhi]).astype(jnp.int32)
    ks_out, own, panel, pattern = assemble(
        place, mask.astype(jnp.float32).reshape(-1), labels_far, arrived_far, collected, core_matrix
    )

    keep = lax.dynamic_index_in_dim(panel, 2 * core + yhi, 0, keepdims=False)
    give = lax.dynamic_index_in_dim(panel, 2 * (1 - core) + yhi, 0, keepdims=False)
    unit = jnp.concatenate([keep, lax.ppermute(give, "core", SWAP)], axis=1)
    b = gather_rows(unit, ylo, x, z)
    densities = []
    for m, a in enumerate(gather_z_whole(own)):
        mask = pattern[512 * m : 512 * m + 512].astype(jnp.float32)
        square = mask * product(a, b)
        a2 = gather_z(square.astype(jnp.bfloat16), m == 0)
        densities.append(3.0 * square - 2.0 * (mask * product(a2, b)))
    return (ks_out, jnp.concatenate(densities, axis=0))


def solution(mesh):
    fine = Mesh(mesh.devices.reshape(2, 4, 8, 2, 2), AXES)
    spread = AXES
    rows, cols = ("ylo", "x"), ("z", "core")
    placed = (
        P(spread, None, None),
        P(spread, None, None),
        P(spread, None),
        P(spread, None),
        P(spread),
        P(rows, cols),
        P(rows, cols),
    )
    return jax.shard_map(
        local,
        mesh=fine,
        in_specs=placed,
        out_specs=(P(rows, cols + ("yhi",)), P(rows, cols + ("yhi",))),
        check_vma=False,
    )
```

```python
import functools
import math

import jax
import jax.numpy as jnp
from jax import lax
from jax.experimental import pallas as pl
from jax.experimental.pallas import tpu as pltpu
from jax.sharding import Mesh
from jax.sharding import PartitionSpec as P

BS = 32
NBLK = 256
COUPLING = 2.5
AXES = ("ylo", "x", "z", "core", "yhi")
SWAP = [(0, 1), (1, 0)]


def lanes_group(shape):
    return lax.broadcasted_iota(jnp.int32, shape, 1) // BS


def pick(pieces, group):
    out = pieces[0]
    for k in range(1, 4):
        out = jnp.where(group == k, pieces[k], out)
    return out


def contribute_kernel(pos_ref, block_ref, left_ref, right_ref, weight_ref, out_ref):
    out_ref[...] = jnp.full(out_ref.shape, 32.0, out_ref.dtype)
    group = lanes_group((8, 128))
    sub = lax.broadcasted_iota(jnp.int32, (8, 128), 0)
    lane = lax.broadcasted_iota(jnp.int32, (8, 128), 1)

    def body(g, carry):
        base = pl.multiple_of(g * 8, 8)
        w = weight_ref[pl.ds(base, 8), :]
        left = left_ref[pl.ds(base, 8)].astype(jnp.float32) * w[:, None, :]
        left = left.astype(jnp.bfloat16).reshape(256, 128)
        right = right_ref[pl.ds(base, 8)].reshape(256, 128)
        for half in range(2):
            c = lax.dot_general(
                left[half * 128 : half * 128 + 128],
                right[half * 128 : half * 128 + 128],
                (((1,), (1,)), ((), ())),
                preferred_element_type=jnp.float32,
            )
            for t in range(4):
                rows = [c[32 * t + 8 * k : 32 * t + 8 * k + 8, :] for k in range(4)]
                rows = [
                    rows[k] if k == t else pltpu.roll(rows[k], (32 * (k - t)) % 128, 1)
                    for k in range(4)
                ]
                task = base + half * 4 + t
                owner, slot = pos_ref[task] >> 1, pos_ref[task] & 1
                out_ref[owner * 3 + slot] = pick(rows, group).astype(jnp.bfloat16)
                block = block_ref[task]
                high = (block >> 4).astype(jnp.float32)
                low = (block & 15).astype(jnp.float32)
                tag = out_ref[owner * 3 + 2].astype(jnp.float32)
                tag = jnp.where(sub == slot, jnp.where(lane == 0, high, low), tag)
                out_ref[owner * 3 + 2] = tag.astype(jnp.bfloat16)
        return carry

    lax.fori_loop(0, 16, body, 0)


def accumulate(acc_ref, label_ref, slot_ref, stride):
    def body(s, carry):
        for u in range(8):
            n = label_ref[s * 8 + u]
            at = (s * 4 + u // 2) * stride + u % 2
            acc_ref[n] = acc_ref[n] + slot_ref[at].astype(jnp.float32)
        return carry

    lax.fori_loop(0, label_ref.shape[0] // 8, body, 0)


def collect_kernel(label_ref, slot_ref, acc_ref):
    acc_ref[...] = jnp.zeros_like(acc_ref)
    accumulate(acc_ref, label_ref, slot_ref, 3)


def assemble_kernel(
    place_ref, mask_ref, label_ref, slot_ref, first_ref, core_ref,
    ks_ref, own_ref, panel_ref, pattern_ref, acc_ref, *, scale,
):
    acc_ref[...] = first_ref[...]
    accumulate(acc_ref, label_ref, slot_ref, 2)
    row, col, half_own = place_ref[0], place_ref[1], place_ref[2]
    group = lanes_group((8, 128))
    sub = lax.broadcasted_iota(jnp.int32, (8, 128), 0)
    lane = lax.broadcasted_iota(jnp.int32, (8, 128), 1)
    slant = sub - lane

    def body(i, carry):
        r0 = pl.multiple_of(i * 32, 32)
        quarter = i // 8
        q0 = pl.multiple_of((i % 8) * 32, 32)
        for side in range(2):
            half = half_own if side == 0 else 1 - half_own
            for jt in range(2):
                n = i * 16 + half * 8 + jt * 4
                blocks = [acc_ref[n + j] for j in range(4)]
                pat = pick([jnp.full((8, 128), mask_ref[n + j]) for j in range(4)], group)
                c0 = pl.multiple_of(half * 256 + jt * 128, 128)
                gap = col * 512 + c0 - row * 1024 - r0
                ks_rows, x_rows = [], []
                for t in range(4):
                    turned = [
                        blocks[j] if j == t else pltpu.roll(blocks[j], (32 * (j - t)) % 128, 1)
                        for j in range(4)
                    ]
                    ks = core_ref[pl.ds(r0 + 8 * t, 8), pl.ds(c0, 128)] + pick(turned, group)
                    identity = jnp.where(slant == gap - 8 * t, 0.5, 0.0)
                    ks_rows.append(ks)
                    x_rows.append(pat * (identity - scale * ks))
                x = jnp.concatenate(x_rows, axis=0).astype(jnp.bfloat16)
                panel_ref[quarter, pl.ds(q0, 32), side * 256 + jt * 128 : side * 256 + jt * 128 + 128] = x
                if side == 0:
                    at = slice(jt * 128, jt * 128 + 128)
                    ks_ref[pl.ds(r0, 32), at] = jnp.concatenate(ks_rows, axis=0)
                    own_ref[pl.ds(r0, 32), at] = x
                    pattern_ref[pl.ds(r0, 32), at] = jnp.concatenate([pat] * 4, axis=0).astype(
                        jnp.bfloat16
                    )
        return carry

    lax.fori_loop(0, 32, body, 0)


VMEM = pl.BlockSpec(memory_space=pltpu.VMEM)
SMEM = pl.BlockSpec(memory_space=pltpu.SMEM)


def contribute(pos, block, left, right, weight):
    tasks = left.shape[0]
    return pl.pallas_call(
        contribute_kernel,
        out_shape=jax.ShapeDtypeStruct((3 * tasks, 8, 128), jnp.bfloat16),
        in_specs=[SMEM, SMEM, VMEM, VMEM, VMEM],
        out_specs=VMEM,
        name="contribute",
    )(pos, block, left, right, weight)


def collect(labels, slots):
    return pl.pallas_call(
        collect_kernel,
        out_shape=jax.ShapeDtypeStruct((520, 8, 128), jnp.float32),
        in_specs=[SMEM, VMEM],
        out_specs=VMEM,
        cost_estimate=pl.CostEstimate(flops=1 << 20, bytes_accessed=1 << 23, transcendentals=0),
        name="collect",
    )(labels, slots)


def assemble(place, mask, labels, slots, first, core):
    return pl.pallas_call(
        functools.partial(assemble_kernel, scale=COUPLING / math.sqrt(NBLK * BS)),
        out_shape=(
            jax.ShapeDtypeStruct((1024, 256), jnp.float32),
            jax.ShapeDtypeStruct((1024, 256), jnp.bfloat16),
            jax.ShapeDtypeStruct((4, 256, 512), jnp.bfloat16),
            jax.ShapeDtypeStruct((1024, 256), jnp.bfloat16),
        ),
        in_specs=[SMEM, SMEM, SMEM, VMEM, VMEM, VMEM],
        out_specs=(VMEM, VMEM, VMEM, VMEM),
        scratch_shapes=[pltpu.VMEM((520, 8, 128), jnp.float32)],
        name="assemble",
    )(place, mask, labels, slots, first, core)


def ring_of(n, step):
    return [(i, (i + step) % n) for i in range(n)]


def gather_z(own, last_up):
    pieces = [own]
    up = down = own
    for s in range(1, 5):
        if s < 4 or last_up:
            up = lax.ppermute(up, "z", ring_of(8, 1))
            pieces.append(up)
        if s < 4 or not last_up:
            down = lax.ppermute(down, "z", ring_of(8, -1))
            pieces.append(down)
    return jnp.stack(pieces)


def place_in_ring(distance):
    distance = distance & 7
    return jnp.where(distance >= 4, 15 - 2 * distance, 2 * distance)


def gather_rows(unit, ylo, x, z):
    fwd, bwd = ring_of(4, 1), ring_of(4, -1)
    near = lax.ppermute(unit, "ylo", SWAP)
    a1 = lax.ppermute(unit, "x", fwd)
    a3 = lax.ppermute(unit, "x", bwd)
    b1, a2 = lax.ppermute(jnp.stack([near, a1]), "x", fwd)
    b3 = lax.ppermute(near, "x", bwd)
    b2 = lax.ppermute(b3, "x", bwd)
    out = jnp.zeros((8,) + unit.shape, unit.dtype)
    for flip, dx, piece in (
        (0, 0, unit), (1, 0, near), (0, 3, a1), (0, 1, a3),
        (1, 3, b1), (1, 1, b3), (0, 2, a2), (1, 2, b2),
    ):
        source = (ylo ^ flip) * 4 + ((x + dx) & 3)
        out = lax.dynamic_update_index_in_dim(out, piece, place_in_ring(source - z), 0)
    return out


def dot(a, b):
    return jnp.einsum("dmk,dkn->mn", a, b, preferred_element_type=jnp.float32)


def product(a, b, chunks):
    far = lax.ppermute(dot(a, b[:, :, 512:]).astype(jnp.bfloat16), "core", SWAP)
    part = dot(a, b[:, :, 256:512]) + far[:, 256:].astype(jnp.float32)
    rest = dot(a, b[:, :, :256]) + far[:, :256].astype(jnp.float32)
    step = part.shape[0] // chunks
    out = []
    for m in range(chunks):
        rows = slice(step * m, step * m + step)
        away = lax.ppermute(part[rows].astype(jnp.bfloat16), "yhi", SWAP)
        out.append((rest[rows], away))
    return out


def local(basis_left, basis_right, grid_weight, task_owner, task_block, core_matrix, block_mask):
    ylo, x, z, core, yhi = (lax.axis_index(a) for a in AXES)
    row, col = ylo * 4 + x, z * 2 + core
    tasks = basis_left.shape[0]

    target = task_owner[:, 0]
    order = jnp.arange(tasks, dtype=jnp.int32)
    earlier = (target[:, None] == target[None, :]) & (order[None, :] < order[:, None])
    pos = target * 2 + jnp.sum(earlier.astype(jnp.int32), axis=1)

    outgoing = contribute(pos, task_block, basis_left, basis_right, grid_weight)
    arrived = lax.all_to_all(
        outgoing.reshape(tasks, 3, 8, 128), AXES[:4], split_axis=0, concat_axis=0, tiled=True
    )
    slots = arrived[:, :2].reshape(2 * tasks, 8, 128)
    tag = arrived[:, 2, :2, :2]
    tag_tile = jnp.pad(tag.reshape(4, 128), ((0, 4), (0, 0)))[None]
    far = lax.ppermute(jnp.concatenate([slots, tag_tile], axis=0), "yhi", SWAP)

    def label_of(tag):
        tag = tag.astype(jnp.float32)
        return jnp.minimum(tag[:, 0] * 16 + tag[:, 1], 512.0).astype(jnp.int32)

    labels = label_of(tag.reshape(2 * tasks, 2))
    labels_far = label_of(far[2 * tasks, :4].reshape(2 * tasks, 2))
    collected = collect(labels, arrived.reshape(3 * tasks, 8, 128))
    block_rows = row * 32 + jnp.arange(32, dtype=jnp.int32)
    block_cols = col * 16 + jnp.arange(16, dtype=jnp.int32)
    mask = (block_mask != 0) | (block_rows[:, None] == block_cols[None, :])
    place = jnp.stack([row, col, yhi]).astype(jnp.int32)
    ks_out, own, panel, pattern = assemble(
        place, mask.astype(jnp.float32).reshape(-1), labels_far, far, collected, core_matrix
    )

    keep = lax.dynamic_index_in_dim(panel, 2 * core + yhi, 0, keepdims=False)
    give = lax.dynamic_index_in_dim(panel, 2 * (1 - core) + yhi, 0, keepdims=False)
    unit = jnp.concatenate([keep, lax.ppermute(give, "core", SWAP)], axis=1)
    b = gather_rows(unit, ylo, x, z)
    squares = []
    for m, (rest, away) in enumerate(product(gather_z(own, True), b, 2)):
        if m > 0:
            away, _ = lax.optimization_barrier((away, squares[0]))
        mask = pattern[512 * m : 512 * m + 512].astype(jnp.float32)
        squares.append(mask * (rest + away.astype(jnp.float32)))
    a2 = [gather_z(square.astype(jnp.bfloat16), m == 0) for m, square in enumerate(squares)]
    ((rest, away),) = product(jnp.concatenate(a2, axis=1), b, 1)
    cube_term = pattern.astype(jnp.float32) * (rest + away.astype(jnp.float32))
    return (ks_out, 3.0 * jnp.concatenate(squares, axis=0) - 2.0 * cube_term)


def solution(mesh):
    fine = Mesh(mesh.devices.reshape(2, 4, 8, 2, 2), AXES)
    spread = AXES
    rows, cols = ("ylo", "x"), ("z", "core")
    placed = (
        P(spread, None, None),
        P(spread, None, None),
        P(spread, None),
        P(spread, None),
        P(spread),
        P(rows, cols),
        P(rows, cols),
    )
    return jax.shard_map(
        local,
        mesh=fine,
        in_specs=placed,
        out_specs=(P(rows, cols + ("yhi",)), P(rows, cols + ("yhi",))),
        check_vma=False,
    )
```

```python
import functools
import math

import jax
import jax.numpy as jnp
from jax import lax
from jax.experimental import pallas as pl
from jax.experimental.pallas import tpu as pltpu
from jax.sharding import Mesh
from jax.sharding import PartitionSpec as P

BS = 32
NBLK = 256
COUPLING = 2.5
AXES = ("ylo", "x", "z", "core", "yhi")
SWAP = [(0, 1), (1, 0)]


def lanes_group(shape):
    return lax.broadcasted_iota(jnp.int32, shape, 1) // BS


def pick(pieces, group):
    out = pieces[0]
    for k in range(1, 4):
        out = jnp.where(group == k, pieces[k], out)
    return out


def contribute_kernel(owner_ref, block_ref, left_ref, right_ref, weight_ref, out_ref, count_ref, tag_ref):
    owners = count_ref.shape[0]
    group = lanes_group((8, 128))
    sub = lax.broadcasted_iota(jnp.int32, (8, 128), 0)
    lane = lax.broadcasted_iota(jnp.int32, (8, 128), 1)

    def clear(o, carry):
        for u in range(8):
            count_ref[o * 8 + u] = 0
            tag_ref[o * 16 + 2 * u] = 512
            tag_ref[o * 16 + 2 * u + 1] = 512
            for slot in range(2):
                out_ref[(o * 8 + u) * 3 + slot] = jnp.zeros((8, 128), jnp.bfloat16)
        return carry

    lax.fori_loop(0, owners // 8, clear, 0)

    def body(g, carry):
        base = pl.multiple_of(g * 16, 16)
        w = weight_ref[pl.ds(base, 16), :]
        left = left_ref[pl.ds(base, 16)].astype(jnp.float32) * w[:, None, :]
        left = left.astype(jnp.bfloat16).reshape(512, 128)
        right = right_ref[pl.ds(base, 16)].reshape(512, 128)
        tiles = []
        for part in range(4):
            c = lax.dot_general(
                left[part * 128 : part * 128 + 128],
                right[part * 128 : part * 128 + 128],
                (((1,), (1,)), ((), ())),
                preferred_element_type=jnp.float32,
            )
            for t in range(4):
                rows = [c[32 * t + 8 * k : 32 * t + 8 * k + 8, :] for k in range(4)]
                rows = [
                    rows[k] if k == t else pltpu.roll(rows[k], (32 * (k - t)) % 128, 1)
                    for k in range(4)
                ]
                tiles.append(pick(rows, group).astype(jnp.bfloat16))
        for t, tile in enumerate(tiles):
            owner = owner_ref[base + t]
            slot = count_ref[owner]
            count_ref[owner] = slot + 1
            tag_ref[owner * 2 + slot] = block_ref[base + t]
            out_ref[owner * 3 + slot] = tile
        return carry

    lax.fori_loop(0, left_ref.shape[0] // 16, body, 0)

    def label(o, carry):
        for u in range(8):
            tags = [tag_ref[o * 16 + 2 * u + slot] for slot in range(2)]
            high = jnp.where(sub == 0, tags[0] >> 4, tags[1] >> 4)
            low = jnp.where(sub == 0, tags[0] & 15, tags[1] & 15)
            tile = jnp.where(lane == 0, high, low).astype(jnp.float32)
            out_ref[(o * 8 + u) * 3 + 2] = tile.astype(jnp.bfloat16)
        return carry

    lax.fori_loop(0, owners // 8, label, 0)


def accumulate(acc_ref, label_ref, slot_ref):
    def body(s, carry):
        for u in range(8):
            n = label_ref[s * 8 + u]
            acc_ref[n] = acc_ref[n] + slot_ref[(s * 4 + u // 2) * 3 + u % 2].astype(jnp.float32)
        return carry

    lax.fori_loop(0, label_ref.shape[0] // 8, body, 0)


def collect_kernel(label_ref, slot_ref, acc_ref):
    acc_ref[...] = jnp.zeros_like(acc_ref)
    accumulate(acc_ref, label_ref, slot_ref)


def assemble_kernel(
    place_ref, mask_ref, label_ref, slot_ref, first_ref, core_ref,
    ks_ref, own_ref, panel_ref, pattern_ref, even_ref, odd_ref, *, scale,
):
    step = pl.program_id(0)

    @pl.when(step == 0)
    def _():
        even_ref[...] = jnp.zeros_like(even_ref)
        odd_ref[...] = jnp.zeros_like(odd_ref)

        def add(s, carry):
            for u in range(4):
                at = s * 8 + 2 * u
                n, m = label_ref[at], label_ref[at + 1]
                even_ref[n] = even_ref[n] + slot_ref[at].astype(jnp.float32)
                odd_ref[m] = odd_ref[m] + slot_ref[at + 1].astype(jnp.float32)
            return carry

        lax.fori_loop(0, label_ref.shape[0] // 8, add, 0)

    row, col, half_own = place_ref[0], place_ref[1], place_ref[2]
    group = lanes_group((8, 128))
    sub = lax.broadcasted_iota(jnp.int32, (8, 128), 0)
    lane = lax.broadcasted_iota(jnp.int32, (8, 128), 1)
    slant = sub - lane

    def body(i, carry):
        r0 = pl.multiple_of(i * 32, 32)
        for side in range(2):
            half = half_own if side == 0 else 1 - half_own
            for jt in range(2):
                near = i * 16 + half * 8 + jt * 4
                n = step * 128 + near
                blocks = [first_ref[near + j] + (even_ref[n + j] + odd_ref[n + j]) for j in range(4)]
                pat = pick([jnp.full((8, 128), mask_ref[n + j]) for j in range(4)], group)
                c0 = pl.multiple_of(half * 256 + jt * 128, 128)
                gap = col * 512 + c0 - row * 1024 - step * 256 - r0
                ks_rows, x_rows = [], []
                for t in range(4):
                    turned = [
                        blocks[j] if j == t else pltpu.roll(blocks[j], (32 * (j - t)) % 128, 1)
                        for j in range(4)
                    ]
                    ks = core_ref[pl.ds(r0 + 8 * t, 8), pl.ds(c0, 128)] + pick(turned, group)
                    identity = jnp.where(slant == gap - 8 * t, 0.5, 0.0)
                    ks_rows.append(ks)
                    x_rows.append(pat * (identity - scale * ks))
                x = jnp.concatenate(x_rows, axis=0).astype(jnp.bfloat16)
                panel_ref[0, pl.ds(r0, 32), side * 256 + jt * 128 : side * 256 + jt * 128 + 128] = x
                if side == 0:
                    at = slice(jt * 128, jt * 128 + 128)
                    ks_ref[pl.ds(r0, 32), at] = jnp.concatenate(ks_rows, axis=0)
                    own_ref[pl.ds(r0, 32), at] = x
                    pattern_ref[pl.ds(r0, 32), at] = jnp.concatenate([pat] * 4, axis=0).astype(
                        jnp.bfloat16
                    )
        return carry

    lax.fori_loop(0, 8, body, 0, unroll=2)


VMEM = pl.BlockSpec(memory_space=pltpu.VMEM)
SMEM = pl.BlockSpec(memory_space=pltpu.SMEM)


def contribute(owner, block, left, right, weight):
    tasks = left.shape[0]
    return pl.pallas_call(
        contribute_kernel,
        out_shape=jax.ShapeDtypeStruct((3 * tasks, 8, 128), jnp.bfloat16),
        in_specs=[SMEM, SMEM, VMEM, VMEM, VMEM],
        out_specs=VMEM,
        scratch_shapes=[pltpu.SMEM((tasks,), jnp.int32), pltpu.SMEM((2 * tasks,), jnp.int32)],
        name="contribute",
    )(owner, block, left, right, weight)


def collect(labels, slots):
    return pl.pallas_call(
        collect_kernel,
        out_shape=jax.ShapeDtypeStruct((520, 8, 128), jnp.float32),
        in_specs=[SMEM, VMEM],
        out_specs=VMEM,
        cost_estimate=pl.CostEstimate(flops=1 << 20, bytes_accessed=1 << 23, transcendentals=0),
        name="collect",
    )(labels, slots)


def assemble(place, mask, labels, slots, first, core):
    def quarter(i):
        return (i, 0)

    return pl.pallas_call(
        functools.partial(assemble_kernel, scale=COUPLING / math.sqrt(NBLK * BS)),
        out_shape=(
            jax.ShapeDtypeStruct((1024, 256), jnp.float32),
            jax.ShapeDtypeStruct((1024, 256), jnp.bfloat16),
            jax.ShapeDtypeStruct((4, 256, 512), jnp.bfloat16),
            jax.ShapeDtypeStruct((1024, 256), jnp.bfloat16),
        ),
        grid=(4,),
        in_specs=[
            SMEM, SMEM, SMEM, VMEM,
            pl.BlockSpec((128, 8, 128), lambda i: (i, 0, 0)),
            pl.BlockSpec((256, 512), quarter),
        ],
        out_specs=(
            pl.BlockSpec((256, 256), quarter),
            pl.BlockSpec((256, 256), quarter),
            pl.BlockSpec((1, 256, 512), lambda i: (i, 0, 0)),
            pl.BlockSpec((256, 256), quarter),
        ),
        scratch_shapes=[pltpu.VMEM((520, 8, 128), jnp.float32)] * 2,
        name="assemble",
    )(place, mask, labels, slots, first, core)


def ring_of(n, step):
    return [(i, (i + step) % n) for i in range(n)]


def gather_z(own, last_up):
    pieces = [own]
    up = down = own
    for s in range(1, 5):
        if s < 4 or last_up:
            up = lax.ppermute(up, "z", ring_of(8, 1))
            pieces.append(up)
        if s < 4 or not last_up:
            down = lax.ppermute(down, "z", ring_of(8, -1))
            pieces.append(down)
    return jnp.stack(pieces)


def place_in_ring(distance):
    distance = distance & 7
    return jnp.where(distance >= 4, 15 - 2 * distance, 2 * distance)


def gather_rows(unit, ylo, x, z):
    fwd, bwd = ring_of(4, 1), ring_of(4, -1)
    near = lax.ppermute(unit, "ylo", SWAP)
    a1 = lax.ppermute(unit, "x", fwd)
    a3 = lax.ppermute(unit, "x", bwd)
    b1, a2 = lax.ppermute(jnp.stack([near, a1]), "x", fwd)
    b3 = lax.ppermute(near, "x", bwd)
    b2 = lax.ppermute(b3, "x", bwd)
    out = jnp.zeros((8,) + unit.shape, unit.dtype)
    for flip, dx, piece in (
        (0, 0, unit), (1, 0, near), (0, 3, a1), (0, 1, a3),
        (1, 3, b1), (1, 1, b3), (0, 2, a2), (1, 2, b2),
    ):
        source = (ylo ^ flip) * 4 + ((x + dx) & 3)
        out = lax.dynamic_update_index_in_dim(out, piece, place_in_ring(source - z), 0)
    return out


def dot(a, b):
    return jnp.einsum("dmk,dkn->mn", a, b, preferred_element_type=jnp.float32)


def product(a, b, chunks):
    far = lax.ppermute(dot(a, b[:, :, 512:]).astype(jnp.bfloat16), "core", SWAP)
    near = lax.optimization_barrier(dot(a, b[:, :, :512]))
    step = a.shape[1] // chunks
    out = []
    for m in range(chunks):
        rows = slice(step * m, step * m + step)
        part = near[rows, 256:] + far[rows, 256:].astype(jnp.float32)
        part = part.astype(jnp.bfloat16)
        if m > 0:
            part, _ = lax.optimization_barrier((part, out[-1][2]))
        away = lax.ppermute(part, "yhi", SWAP)
        out.append((near[rows, :256], far[rows, :256], away))
    return out


def local(basis_left, basis_right, grid_weight, task_owner, task_block, core_matrix, block_mask):
    ylo, x, z, core, yhi = (lax.axis_index(a) for a in AXES)
    row, col = ylo * 4 + x, z * 2 + core
    tasks = basis_left.shape[0]

    outgoing = contribute(task_owner[:, 0], task_block, basis_left, basis_right, grid_weight)
    arrived = lax.all_to_all(
        outgoing.reshape(tasks, 3, 8, 128), AXES[:4], split_axis=0, concat_axis=0, tiled=True
    )
    slots = arrived[:, :2].reshape(2 * tasks, 8, 128)
    tag = arrived[:, 2, :2, :2]
    tag_tile = jnp.pad(tag.reshape(4, 128), ((0, 4), (0, 0)))[None]
    far = lax.ppermute(jnp.concatenate([slots, tag_tile], axis=0), "yhi", SWAP)

    def label_of(tag):
        tag = tag.astype(jnp.float32)
        return jnp.minimum(tag[:, 0] * 16 + tag[:, 1], 512.0).astype(jnp.int32)

    labels = label_of(tag.reshape(2 * tasks, 2))
    labels_far = label_of(far[2 * tasks, :4].reshape(2 * tasks, 2))
    collected = collect(labels, arrived.reshape(3 * tasks, 8, 128))
    block_rows = row * 32 + jnp.arange(32, dtype=jnp.int32)
    block_cols = col * 16 + jnp.arange(16, dtype=jnp.int32)
    mask = (block_mask != 0) | (block_rows[:, None] == block_cols[None, :])
    place = jnp.stack([row, col, yhi]).astype(jnp.int32)
    ks_out, own, panel, pattern = assemble(
        place, mask.astype(jnp.float32).reshape(-1), labels_far, far, collected, core_matrix
    )

    keep = lax.dynamic_index_in_dim(panel, 2 * core + yhi, 0, keepdims=False)
    give = lax.dynamic_index_in_dim(panel, 2 * (1 - core) + yhi, 0, keepdims=False)
    unit = jnp.concatenate([keep, lax.ppermute(give, "core", SWAP)], axis=1)
    b = gather_rows(unit, ylo, x, z)
    squares = []
    for m, (near, far, away) in enumerate(product(gather_z(own, True), b, 2)):
        if m > 0:
            away, _ = lax.optimization_barrier((away, squares[0]))
        mask = pattern[512 * m : 512 * m + 512].astype(jnp.float32)
        squares.append(mask * (near + far.astype(jnp.float32) + away.astype(jnp.float32)))
    a2 = [gather_z(square.astype(jnp.bfloat16), m == 0) for m, square in enumerate(squares)]
    ((near, far, away),) = product(jnp.concatenate(a2, axis=1), b, 1)
    cube_term = pattern.astype(jnp.float32) * (near + far.astype(jnp.float32) + away.astype(jnp.float32))
    return (ks_out, 3.0 * jnp.concatenate(squares, axis=0) - 2.0 * cube_term)


def solution(mesh):
    fine = Mesh(mesh.devices.reshape(2, 4, 8, 2, 2), AXES)
    spread = AXES
    rows, cols = ("ylo", "x"), ("z", "core")
    placed = (
        P(spread, None, None),
        P(spread, None, None),
        P(spread, None),
        P(spread, None),
        P(spread),
        P(rows, cols),
        P(rows, cols),
    )
    return jax.shard_map(
        local,
        mesh=fine,
        in_specs=placed,
        out_specs=(P(rows, cols + ("yhi",)), P(rows, cols + ("yhi",))),
        check_vma=False,
    )
```

```python
import functools
import math

import jax
import jax.numpy as jnp
from jax import lax
from jax.experimental import pallas as pl
from jax.experimental.pallas import tpu as pltpu
from jax.sharding import Mesh
from jax.sharding import PartitionSpec as P

BS = 32
NBLK = 256
COUPLING = 2.5
AXES = ("ylo", "x", "z", "core", "yhi")
SWAP = [(0, 1), (1, 0)]


def lanes_group(shape):
    return lax.broadcasted_iota(jnp.int32, shape, 1) // BS


def pick(pieces, group):
    out = pieces[0]
    for k in range(1, 4):
        out = jnp.where(group == k, pieces[k], out)
    return out


def contribute_kernel(owner_ref, block_ref, left_ref, right_ref, weight_ref, out_ref, count_ref, tag_ref):
    owners = count_ref.shape[0]
    group = lanes_group((8, 128))
    sub = lax.broadcasted_iota(jnp.int32, (2, 128), 0)
    lane = lax.broadcasted_iota(jnp.int32, (2, 128), 1)

    def clear(o, carry):
        for u in range(8):
            count_ref[o * 8 + u] = 0
            tag_ref[o * 16 + 2 * u] = 512
            tag_ref[o * 16 + 2 * u + 1] = 512
            out_ref[o * 8 + u] = jnp.zeros((9, 2, 128), jnp.bfloat16)
        return carry

    lax.fori_loop(0, owners // 8, clear, 0)

    def body(g, carry):
        base = pl.multiple_of(g * 16, 16)
        w = weight_ref[pl.ds(base, 16), :]
        left = left_ref[pl.ds(base, 16)].astype(jnp.float32) * w[:, None, :]
        left = left.astype(jnp.bfloat16).reshape(512, 128)
        right = right_ref[pl.ds(base, 16)].reshape(512, 128)
        tiles = []
        for part in range(4):
            c = lax.dot_general(
                left[part * 128 : part * 128 + 128],
                right[part * 128 : part * 128 + 128],
                (((1,), (1,)), ((), ())),
                preferred_element_type=jnp.float32,
            )
            for t in range(4):
                rows = [c[32 * t + 8 * k : 32 * t + 8 * k + 8, :] for k in range(4)]
                rows = [
                    rows[k] if k == t else pltpu.roll(rows[k], (32 * (k - t)) % 128, 1)
                    for k in range(4)
                ]
                tiles.append(pick(rows, group).reshape(4, 2, 128).astype(jnp.bfloat16))
        for t, tile in enumerate(tiles):
            owner = owner_ref[base + t]
            slot = count_ref[owner]
            count_ref[owner] = slot + 1
            tag_ref[owner * 2 + slot] = block_ref[base + t]
            out_ref[owner, pl.ds(slot * 4, 4)] = tile
        return carry

    lax.fori_loop(0, left_ref.shape[0] // 16, body, 0)

    def label(o, carry):
        for u in range(8):
            tags = [tag_ref[o * 16 + 2 * u + slot] for slot in range(2)]
            high = jnp.where(sub == 0, tags[0] >> 4, tags[1] >> 4)
            low = jnp.where(sub == 0, tags[0] & 15, tags[1] & 15)
            tile = jnp.where(lane == 0, high, low).astype(jnp.float32)
            out_ref[o * 8 + u, 8] = tile.astype(jnp.bfloat16)
        return carry

    lax.fori_loop(0, owners // 8, label, 0)


def accumulate(acc_ref, label_ref, slot_ref):
    def body(s, carry):
        for u in range(8):
            n = label_ref[s * 8 + u]
            acc_ref[n] = acc_ref[n] + slot_ref[s * 8 + u].astype(jnp.float32)
        return carry

    lax.fori_loop(0, label_ref.shape[0] // 8, body, 0)


def collect_kernel(label_ref, slot_ref, acc_ref):
    acc_ref[...] = jnp.zeros_like(acc_ref)
    accumulate(acc_ref, label_ref, slot_ref)


def assemble_kernel(
    place_ref, mask_ref, label_ref, slot_ref, first_ref, core_ref,
    ks_ref, own_ref, panel_ref, pattern_ref, even_ref, odd_ref, *, scale,
):
    step = pl.program_id(0)

    @pl.when(step == 0)
    def _():
        even_ref[...] = jnp.zeros_like(even_ref)
        odd_ref[...] = jnp.zeros_like(odd_ref)

        def add(s, carry):
            for u in range(4):
                at = s * 8 + 2 * u
                n, m = label_ref[at], label_ref[at + 1]
                even_ref[n] = even_ref[n] + slot_ref[at].astype(jnp.float32)
                odd_ref[m] = odd_ref[m] + slot_ref[at + 1].astype(jnp.float32)
            return carry

        lax.fori_loop(0, label_ref.shape[0] // 8, add, 0)

    row, col, half_own = place_ref[0], place_ref[1], place_ref[2]
    apart = step ^ (2 * (col & 1) + half_own)
    kept = jnp.where(apart == 0, 0, jnp.where(apart == 2, 1, 2))
    group = lanes_group((8, 128))
    sub = lax.broadcasted_iota(jnp.int32, (8, 128), 0)
    lane = lax.broadcasted_iota(jnp.int32, (8, 128), 1)
    slant = sub - lane

    def body(i, carry):
        r0 = pl.multiple_of(i * 32, 32)
        for side in range(2):
            half = half_own if side == 0 else 1 - half_own
            for jt in range(2):
                near = i * 16 + half * 8 + jt * 4
                n = step * 128 + near
                blocks = [first_ref[near + j] + (even_ref[n + j] + odd_ref[n + j]) for j in range(4)]
                pat = pick([jnp.full((8, 128), mask_ref[n + j]) for j in range(4)], group)
                c0 = pl.multiple_of(half * 256 + jt * 128, 128)
                gap = col * 512 + c0 - row * 1024 - step * 256 - r0
                ks_rows, x_rows = [], []
                for t in range(4):
                    turned = [
                        blocks[j] if j == t else pltpu.roll(blocks[j], (32 * (j - t)) % 128, 1)
                        for j in range(4)
                    ]
                    ks = core_ref[pl.ds(r0 + 8 * t, 8), pl.ds(c0, 128)] + pick(turned, group)
                    identity = jnp.where(slant == gap - 8 * t, 0.5, 0.0)
                    ks_rows.append(ks)
                    x_rows.append(pat * (identity - scale * ks))
                x = jnp.concatenate(x_rows, axis=0).astype(jnp.bfloat16)
                panel_ref[kept, pl.ds(r0, 32), side * 256 + jt * 128 : side * 256 + jt * 128 + 128] = x
                if side == 0:
                    at = slice(jt * 128, jt * 128 + 128)
                    ks_ref[pl.ds(r0, 32), at] = jnp.concatenate(ks_rows, axis=0)
                    own_ref[pl.ds(r0, 32), at] = x
                    pattern_ref[pl.ds(r0, 32), at] = jnp.concatenate([pat] * 4, axis=0).astype(
                        jnp.bfloat16
                    )
        return carry

    lax.fori_loop(0, 8, body, 0, unroll=2)


VMEM = pl.BlockSpec(memory_space=pltpu.VMEM)
SMEM = pl.BlockSpec(memory_space=pltpu.SMEM)


def contribute(owner, block, left, right, weight):
    tasks = left.shape[0]
    return pl.pallas_call(
        contribute_kernel,
        out_shape=jax.ShapeDtypeStruct((tasks, 9, 2, 128), jnp.bfloat16),
        in_specs=[SMEM, SMEM, VMEM, VMEM, VMEM],
        out_specs=VMEM,
        scratch_shapes=[pltpu.SMEM((tasks,), jnp.int32), pltpu.SMEM((2 * tasks,), jnp.int32)],
        name="contribute",
    )(owner, block, left, right, weight)


def collect(labels, slots):
    return pl.pallas_call(
        collect_kernel,
        out_shape=jax.ShapeDtypeStruct((520, 8, 128), jnp.float32),
        in_specs=[SMEM, VMEM],
        out_specs=VMEM,
        cost_estimate=pl.CostEstimate(flops=1 << 20, bytes_accessed=1 << 23, transcendentals=0),
        name="collect",
    )(labels, slots)


def assemble(place, mask, labels, slots, first, core):
    def quarter(i):
        return (i, 0)

    return pl.pallas_call(
        functools.partial(assemble_kernel, scale=COUPLING / math.sqrt(NBLK * BS)),
        out_shape=(
            jax.ShapeDtypeStruct((1024, 256), jnp.float32),
            jax.ShapeDtypeStruct((1024, 256), jnp.bfloat16),
            jax.ShapeDtypeStruct((3, 256, 512), jnp.bfloat16),
            jax.ShapeDtypeStruct((1024, 256), jnp.bfloat16),
        ),
        grid=(4,),
        in_specs=[
            SMEM, SMEM, SMEM, VMEM,
            pl.BlockSpec((128, 8, 128), lambda i: (i, 0, 0)),
            pl.BlockSpec((256, 512), quarter),
        ],
        out_specs=(
            pl.BlockSpec((256, 256), quarter),
            pl.BlockSpec((256, 256), quarter),
            pl.BlockSpec((3, 256, 512), lambda i: (0, 0, 0)),
            pl.BlockSpec((256, 256), quarter),
        ),
        scratch_shapes=[pltpu.VMEM((520, 8, 128), jnp.float32)] * 2,
        name="assemble",
    )(place, mask, labels, slots, first, core)


def ring_of(n, step):
    return [(i, (i + step) % n) for i in range(n)]


def gather_z(own, last_up):
    pieces = [own]
    up = down = own
    for s in range(1, 5):
        if s < 4 or last_up:
            up = lax.ppermute(up, "z", ring_of(8, 1))
            pieces.append(up)
        if s < 4 or not last_up:
            down = lax.ppermute(down, "z", ring_of(8, -1))
            pieces.append(down)
    return jnp.stack(pieces)


def place_in_ring(distance):
    distance = distance & 7
    return jnp.where(distance >= 4, 15 - 2 * distance, 2 * distance)


def gather_rows(unit, ylo, x, z):
    fwd, bwd = ring_of(4, 1), ring_of(4, -1)
    near = lax.ppermute(unit, "ylo", SWAP)
    a1 = lax.ppermute(unit, "x", fwd)
    a3 = lax.ppermute(unit, "x", bwd)
    b1, a2 = lax.ppermute(jnp.stack([near, a1]), "x", fwd)
    b3 = lax.ppermute(near, "x", bwd)
    b2 = lax.ppermute(b3, "x", bwd)
    out = jnp.zeros((8,) + unit.shape, unit.dtype)
    for flip, dx, piece in (
        (0, 0, unit), (1, 0, near), (0, 3, a1), (0, 1, a3),
        (1, 3, b1), (1, 1, b3), (0, 2, a2), (1, 2, b2),
    ):
        source = (ylo ^ flip) * 4 + ((x + dx) & 3)
        out = lax.dynamic_update_index_in_dim(out, piece, place_in_ring(source - z), 0)
    return out


def dot(a, b):
    return jnp.einsum("dmk,dkn->mn", a, b, preferred_element_type=jnp.float32)


def product(a, b, chunks):
    far = lax.ppermute(dot(a, b[:, :, 512:]).astype(jnp.bfloat16), "core", SWAP)
    near = lax.optimization_barrier(dot(a, b[:, :, :512]))
    step = a.shape[1] // chunks
    out = []
    for m in range(chunks):
        rows = slice(step * m, step * m + step)
        part = near[rows, 256:] + far[rows, 256:].astype(jnp.float32)
        part = part.astype(jnp.bfloat16)
        if m > 0:
            part, _ = lax.optimization_barrier((part, out[-1][2]))
        away = lax.ppermute(part, "yhi", SWAP)
        out.append((near[rows, :256], far[rows, :256], away))
    return out


def local(basis_left, basis_right, grid_weight, task_owner, task_block, core_matrix, block_mask):
    ylo, x, z, core, yhi = (lax.axis_index(a) for a in AXES)
    row, col = ylo * 4 + x, z * 2 + core
    tasks = basis_left.shape[0]

    outgoing = contribute(task_owner[:, 0], task_block, basis_left, basis_right, grid_weight)
    arrived = lax.all_to_all(
        outgoing, AXES[:4], split_axis=0, concat_axis=0, tiled=True
    )
    slots = arrived[:, :8].reshape(2 * tasks, 8, 128)
    tag = arrived[:, 8, :, :2]
    tag_tile = jnp.pad(tag.reshape(4, 128), ((0, 4), (0, 0)))[None]
    slots = jnp.concatenate([slots, tag_tile], axis=0)
    far = lax.ppermute(slots, "yhi", SWAP)

    def label_of(tag):
        tag = tag.astype(jnp.float32)
        return jnp.minimum(tag[:, 0] * 16 + tag[:, 1], 512.0).astype(jnp.int32)

    labels = label_of(tag.reshape(2 * tasks, 2))
    labels_far = label_of(far[2 * tasks, :4].reshape(2 * tasks, 2))
    collected = collect(labels, slots)
    block_rows = row * 32 + jnp.arange(32, dtype=jnp.int32)
    block_cols = col * 16 + jnp.arange(16, dtype=jnp.int32)
    mask = (block_mask != 0) | (block_rows[:, None] == block_cols[None, :])
    place = jnp.stack([row, col, yhi]).astype(jnp.int32)
    ks_out, own, panel, pattern = assemble(
        place, mask.astype(jnp.float32).reshape(-1), labels_far, far, collected, core_matrix
    )

    keep, give = panel[0], panel[1]
    unit = jnp.concatenate([keep, lax.ppermute(give, "core", SWAP)], axis=1)
    b = gather_rows(unit, ylo, x, z)
    squares = []
    for m, (near, far, away) in enumerate(product(gather_z(own, True), b, 2)):
        if m > 0:
            away, _ = lax.optimization_barrier((away, squares[0]))
        mask = pattern[512 * m : 512 * m + 512].astype(jnp.float32)
        squares.append(mask * (near + far.astype(jnp.float32) + away.astype(jnp.float32)))
    a2 = [gather_z(square.astype(jnp.bfloat16), m == 0) for m, square in enumerate(squares)]
    ((near, far, away),) = product(jnp.concatenate(a2, axis=1), b, 1)
    cube_term = pattern.astype(jnp.float32) * (near + far.astype(jnp.float32) + away.astype(jnp.float32))
    return (ks_out, 3.0 * jnp.concatenate(squares, axis=0) - 2.0 * cube_term)


def solution(mesh):
    fine = Mesh(mesh.devices.reshape(2, 4, 8, 2, 2), AXES)
    spread = AXES
    rows, cols = ("ylo", "x"), ("z", "core")
    placed = (
        P(spread, None, None),
        P(spread, None, None),
        P(spread, None),
        P(spread, None),
        P(spread),
        P(rows, cols),
        P(rows, cols),
    )
    return jax.shard_map(
        local,
        mesh=fine,
        in_specs=placed,
        out_specs=(P(rows, cols + ("yhi",)), P(rows, cols + ("yhi",))),
        check_vma=False,
    )
```

```python
import functools
import math

import jax
import jax.numpy as jnp
from jax import lax
from jax.experimental import pallas as pl
from jax.experimental.pallas import tpu as pltpu
from jax.sharding import Mesh
from jax.sharding import PartitionSpec as P

BS = 32
NBLK = 256
COUPLING = 2.5
AXES = ("ylo", "x", "z", "core", "yhi")
SWAP = [(0, 1), (1, 0)]


def lanes_group(shape):
    return lax.broadcasted_iota(jnp.int32, shape, 1) // BS


def pick(pieces, group):
    out = pieces[0]
    for k in range(1, 4):
        out = jnp.where(group == k, pieces[k], out)
    return out


def contribute_kernel(owner_ref, block_ref, left_ref, right_ref, weight_ref, out_ref, count_ref, tag_ref):
    owners = count_ref.shape[0]
    group = lanes_group((8, 128))
    sub = lax.broadcasted_iota(jnp.int32, (2, 128), 0)
    lane = lax.broadcasted_iota(jnp.int32, (2, 128), 1)

    def clear(o, carry):
        for u in range(8):
            count_ref[o * 8 + u] = 0
            tag_ref[o * 16 + 2 * u] = 512
            tag_ref[o * 16 + 2 * u + 1] = 512
            out_ref[o * 8 + u] = jnp.zeros((9, 2, 128), jnp.bfloat16)
        return carry

    lax.fori_loop(0, owners // 8, clear, 0)

    def body(g, carry):
        base = pl.multiple_of(g * 16, 16)
        w = weight_ref[pl.ds(base, 16), :]
        left = left_ref[pl.ds(base, 16)].astype(jnp.float32) * w[:, None, :]
        left = left.astype(jnp.bfloat16).reshape(512, 128)
        right = right_ref[pl.ds(base, 16)].reshape(512, 128)
        tiles = []
        for part in range(4):
            c = lax.dot_general(
                left[part * 128 : part * 128 + 128],
                right[part * 128 : part * 128 + 128],
                (((1,), (1,)), ((), ())),
                preferred_element_type=jnp.float32,
            )
            for t in range(4):
                rows = [c[32 * t + 8 * k : 32 * t + 8 * k + 8, :] for k in range(4)]
                rows = [
                    rows[k] if k == t else pltpu.roll(rows[k], (32 * (k - t)) % 128, 1)
                    for k in range(4)
                ]
                tiles.append(pick(rows, group).reshape(4, 2, 128).astype(jnp.bfloat16))
        for t, tile in enumerate(tiles):
            owner = owner_ref[base + t]
            slot = count_ref[owner]
            count_ref[owner] = slot + 1
            tag_ref[owner * 2 + slot] = block_ref[base + t]
            out_ref[owner, pl.ds(slot * 4, 4)] = tile
        return carry

    lax.fori_loop(0, left_ref.shape[0] // 16, body, 0)

    def label(o, carry):
        for u in range(8):
            tags = [tag_ref[o * 16 + 2 * u + slot] for slot in range(2)]
            high = jnp.where(sub == 0, tags[0] >> 4, tags[1] >> 4)
            low = jnp.where(sub == 0, tags[0] & 15, tags[1] & 15)
            tile = jnp.where(lane == 0, high, low).astype(jnp.float32)
            out_ref[o * 8 + u, 8] = tile.astype(jnp.bfloat16)
        return carry

    lax.fori_loop(0, owners // 8, label, 0)


def read_labels(slot_ref, vector_ref, label_ref):
    pairs = slot_ref[slot_ref.shape[0] - 1].astype(jnp.float32)
    labels = jnp.minimum(pairs * 16.0 + pltpu.roll(pairs, 127, 1), 512.0)
    vector_ref[...] = labels.astype(jnp.int32)
    pltpu.sync_copy(vector_ref, label_ref)


def add_slots(even_ref, odd_ref, label_ref, slot_ref):
    even_ref[...] = jnp.zeros_like(even_ref)
    odd_ref[...] = jnp.zeros_like(odd_ref)

    def add(s, carry):
        for u in range(4):
            at = s * 8 + 2 * u
            place = (s % 8) * 16 + 4 * u
            n, m = label_ref[s // 8, place], label_ref[s // 8, place + 2]
            even_ref[n] = even_ref[n] + slot_ref[at].astype(jnp.float32)
            odd_ref[m] = odd_ref[m] + slot_ref[at + 1].astype(jnp.float32)
        return carry

    lax.fori_loop(0, slot_ref.shape[0] // 8, add, 0)


def spread(blocks, group):
    rows = []
    for t in range(4):
        turned = [
            blocks[j] if j == t else pltpu.roll(blocks[j], (32 * (j - t)) % 128, 1) for j in range(4)
        ]
        rows.append(pick(turned, group))
    return rows


def where_am_i():
    ylo, x, z, core, yhi = (lax.axis_index(a) for a in AXES)
    return ylo * 4 + x, z * 2 + core, yhi


def collect_kernel(
    mask_ref, slot_ref, core_ref, base_ref, pattern_ref, even_ref, odd_ref, vector_ref, label_ref
):
    read_labels(slot_ref, vector_ref, label_ref)
    add_slots(even_ref, odd_ref, label_ref, slot_ref)
    row, col, half_own = where_am_i()
    group = lanes_group((8, 128))

    def body(i, carry):
        r0 = pl.multiple_of(i * 32, 32)
        for side in range(2):
            half = half_own if side == 0 else 1 - half_own
            for jt in range(2):
                j0 = half * 8 + jt * 4
                n = i * 16 + j0
                blocks = [even_ref[n + j] + odd_ref[n + j] for j in range(4)]
                marks = []
                for j in range(4):
                    on = (mask_ref[i, j0 + j] != 0) | (row * 32 + i == col * 16 + j0 + j)
                    marks.append(jnp.full((8, 128), jnp.where(on, 1.0, 0.0)))
                pat = pick(marks, group)
                c0 = pl.multiple_of(half * 256 + jt * 128, 128)
                at = slice(side * 256 + jt * 128, side * 256 + jt * 128 + 128)
                base_ref[pl.ds(r0, 32), at] = core_ref[pl.ds(r0, 32), pl.ds(c0, 128)] + (
                    jnp.concatenate(spread(blocks, group), axis=0)
                )
                pattern_ref[pl.ds(r0, 32), at] = jnp.concatenate([pat] * 4, axis=0).astype(jnp.bfloat16)
        return carry

    lax.fori_loop(0, 32, body, 0)


def assemble_kernel(
    slot_ref, base_ref, pattern_ref, ks_ref, own_ref, panel_ref,
    even_ref, odd_ref, vector_ref, label_ref, *, scale,
):
    step = pl.program_id(0)

    @pl.when(step == 0)
    def _():
        read_labels(slot_ref, vector_ref, label_ref)
        add_slots(even_ref, odd_ref, label_ref, slot_ref)

    row, col, half_own = where_am_i()
    apart = step ^ (2 * (col & 1) + half_own)
    kept = jnp.where(apart == 0, 0, jnp.where(apart == 2, 1, 2))
    group = lanes_group((8, 128))
    slant = lax.broadcasted_iota(jnp.int32, (32, 128), 0) - lax.broadcasted_iota(jnp.int32, (32, 128), 1)

    def body(i, carry):
        r0 = pl.multiple_of(i * 32, 32)
        for side in range(2):
            half = half_own if side == 0 else 1 - half_own
            for jt in range(2):
                n = step * 128 + i * 16 + half * 8 + jt * 4
                blocks = [even_ref[n + j] + odd_ref[n + j] for j in range(4)]
                at = slice(side * 256 + jt * 128, side * 256 + jt * 128 + 128)
                ks = base_ref[pl.ds(r0, 32), at] + jnp.concatenate(spread(blocks, group), axis=0)
                gap = col * 512 + half * 256 + jt * 128 - row * 1024 - step * 256 - r0
                identity = jnp.where(slant == gap, 0.5, 0.0)
                pat = pattern_ref[pl.ds(r0, 32), at].astype(jnp.float32)
                x = (pat * (identity - scale * ks)).astype(jnp.bfloat16)
                panel_ref[kept, pl.ds(r0, 32), at] = x
                if side == 0:
                    ks_ref[pl.ds(r0, 32), at] = ks
                    own_ref[pl.ds(r0, 32), at] = x
        return carry

    lax.fori_loop(0, 8, body, 0, unroll=2)


VMEM = pl.BlockSpec(memory_space=pltpu.VMEM)
SMEM = pl.BlockSpec(memory_space=pltpu.SMEM)


def contribute(owner, block, left, right, weight):
    tasks = left.shape[0]
    return pl.pallas_call(
        contribute_kernel,
        out_shape=jax.ShapeDtypeStruct((tasks, 9, 2, 128), jnp.bfloat16),
        in_specs=[SMEM, SMEM, VMEM, VMEM, VMEM],
        out_specs=VMEM,
        scratch_shapes=[pltpu.SMEM((tasks,), jnp.int32), pltpu.SMEM((2 * tasks,), jnp.int32)],
        name="contribute",
    )(owner, block, left, right, weight)


ADDERS = [
    pltpu.VMEM((520, 8, 128), jnp.float32),
    pltpu.VMEM((520, 8, 128), jnp.float32),
    pltpu.VMEM((8, 128), jnp.int32),
    pltpu.SMEM((8, 128), jnp.int32),
]


def collect(mask, slots, core):
    return pl.pallas_call(
        collect_kernel,
        out_shape=(
            jax.ShapeDtypeStruct((1024, 512), jnp.float32),
            jax.ShapeDtypeStruct((1024, 512), jnp.bfloat16),
        ),
        in_specs=[SMEM, VMEM, VMEM],
        out_specs=(VMEM, VMEM),
        scratch_shapes=ADDERS,
        cost_estimate=pl.CostEstimate(flops=1 << 20, bytes_accessed=1 << 23, transcendentals=0),
        name="collect",
    )(mask, slots, core)


def assemble(slots, base, pattern):
    def quarter(i):
        return (i, 0)

    return pl.pallas_call(
        functools.partial(assemble_kernel, scale=COUPLING / math.sqrt(NBLK * BS)),
        out_shape=(
            jax.ShapeDtypeStruct((1024, 256), jnp.float32),
            jax.ShapeDtypeStruct((1024, 256), jnp.bfloat16),
            jax.ShapeDtypeStruct((3, 256, 512), jnp.bfloat16),
        ),
        grid=(4,),
        in_specs=[VMEM, pl.BlockSpec((256, 512), quarter), pl.BlockSpec((256, 512), quarter)],
        out_specs=(
            pl.BlockSpec((256, 256), quarter),
            pl.BlockSpec((256, 256), quarter),
            pl.BlockSpec((3, 256, 512), lambda i: (0, 0, 0)),
        ),
        scratch_shapes=ADDERS,
        name="assemble",
    )(slots, base, pattern)


def ring_of(n, step):
    return [(i, (i + step) % n) for i in range(n)]


def gather_z(own, last_up):
    pieces = [own]
    up = down = own
    for s in range(1, 5):
        if s < 4 or last_up:
            up = lax.ppermute(up, "z", ring_of(8, 1))
            pieces.append(up)
        if s < 4 or not last_up:
            down = lax.ppermute(down, "z", ring_of(8, -1))
            pieces.append(down)
    return jnp.stack(pieces)


def place_in_ring(distance):
    distance = distance & 7
    return jnp.where(distance >= 4, 15 - 2 * distance, 2 * distance)


def gather_rows(unit, ylo, x, z):
    fwd, bwd = ring_of(4, 1), ring_of(4, -1)
    near = lax.ppermute(unit, "ylo", SWAP)
    a1 = lax.ppermute(unit, "x", fwd)
    a3 = lax.ppermute(unit, "x", bwd)
    b1, a2 = lax.ppermute(jnp.stack([near, a1]), "x", fwd)
    b3 = lax.ppermute(near, "x", bwd)
    b2 = lax.ppermute(b3, "x", bwd)
    out = jnp.zeros((8,) + unit.shape, unit.dtype)
    for flip, dx, piece in (
        (0, 0, unit), (1, 0, near), (0, 3, a1), (0, 1, a3),
        (1, 3, b1), (1, 1, b3), (0, 2, a2), (1, 2, b2),
    ):
        source = (ylo ^ flip) * 4 + ((x + dx) & 3)
        out = lax.dynamic_update_index_in_dim(out, piece, place_in_ring(source - z), 0)
    return out


def dot(a, b):
    return jnp.einsum("dmk,dkn->mn", a, b, preferred_element_type=jnp.float32)


def product(a, b, chunks):
    far = lax.ppermute(dot(a, b[:, :, 512:]).astype(jnp.bfloat16), "core", SWAP)
    near = lax.optimization_barrier(dot(a, b[:, :, :512]))
    step = a.shape[1] // chunks
    out = []
    for m in range(chunks):
        rows = slice(step * m, step * m + step)
        part = near[rows, 256:] + far[rows, 256:].astype(jnp.float32)
        part = part.astype(jnp.bfloat16)
        if m > 0:
            part, _ = lax.optimization_barrier((part, out[-1][2]))
        away = lax.ppermute(part, "yhi", SWAP)
        out.append((near[rows, :256], far[rows, :256], away))
    return out


def local(basis_left, basis_right, grid_weight, task_owner, task_block, core_matrix, block_mask):
    ylo, x, z = (lax.axis_index(a) for a in AXES[:3])
    tasks = basis_left.shape[0]

    outgoing = contribute(task_owner[:, 0], task_block, basis_left, basis_right, grid_weight)
    arrived = lax.all_to_all(
        outgoing, AXES[:4], split_axis=0, concat_axis=0, tiled=True
    )
    slots = arrived[:, :8].reshape(2 * tasks, 8, 128)
    tag = arrived[:, 8, :, :2]
    tag_tile = jnp.pad(tag.reshape(4, 128), ((0, 4), (0, 0)))[None]
    slots = jnp.concatenate([slots, tag_tile], axis=0)
    far = lax.ppermute(slots, "yhi", SWAP)

    base, pattern = collect(block_mask, slots, core_matrix)
    ks_out, own, panel = assemble(far, base, pattern)

    keep, give = panel[0], lax.ppermute(panel[1], "core", SWAP)
    unit = jnp.concatenate([keep, give], axis=1)
    b = gather_rows(unit, ylo, x, z)
    squares = []
    for m, (near, far, away) in enumerate(product(gather_z(own, True), b, 2)):
        if m > 0:
            away, _ = lax.optimization_barrier((away, squares[0]))
        mask = pattern[512 * m : 512 * m + 512, :256].astype(jnp.float32)
        squares.append(mask * (near + far.astype(jnp.float32) + away.astype(jnp.float32)))
    a2 = [gather_z(square.astype(jnp.bfloat16), m == 0) for m, square in enumerate(squares)]
    ((near, far, away),) = product(jnp.concatenate(a2, axis=1), b, 1)
    cube_term = pattern[:, :256].astype(jnp.float32) * (near + far.astype(jnp.float32) + away.astype(jnp.float32))
    return (ks_out, 3.0 * jnp.concatenate(squares, axis=0) - 2.0 * cube_term)


def solution(mesh):
    fine = Mesh(mesh.devices.reshape(2, 4, 8, 2, 2), AXES)
    spread = AXES
    rows, cols = ("ylo", "x"), ("z", "core")
    placed = (
        P(spread, None, None),
        P(spread, None, None),
        P(spread, None),
        P(spread, None),
        P(spread),
        P(rows, cols),
        P(rows, cols),
    )
    return jax.shard_map(
        local,
        mesh=fine,
        in_specs=placed,
        out_specs=(P(rows, cols + ("yhi",)), P(rows, cols + ("yhi",))),
        check_vma=False,
    )
```

```python
import functools
import math

import jax
import jax.numpy as jnp
from jax import lax
from jax.experimental import pallas as pl
from jax.experimental.pallas import tpu as pltpu
from jax.sharding import Mesh
from jax.sharding import PartitionSpec as P

BS = 32
NBLK = 256
COUPLING = 2.5
AXES = ("ylo", "x", "z", "core", "yhi")
SWAP = [(0, 1), (1, 0)]


def lanes_group(shape):
    return lax.broadcasted_iota(jnp.int32, shape, 1) // BS


def pick(pieces, group):
    out = pieces[0]
    for k in range(1, 4):
        out = jnp.where(group == k, pieces[k], out)
    return out


def contribute_kernel(owner_ref, block_ref, left_ref, right_ref, weight_ref, out_ref, count_ref, tag_ref):
    owners = count_ref.shape[0]
    group = lanes_group((8, 128))
    sub = lax.broadcasted_iota(jnp.int32, (2, 128), 0)
    lane = lax.broadcasted_iota(jnp.int32, (2, 128), 1)

    def clear(o, carry):
        for u in range(8):
            count_ref[o * 8 + u] = 0
            tag_ref[o * 16 + 2 * u] = 512
            tag_ref[o * 16 + 2 * u + 1] = 512
            out_ref[o * 8 + u] = jnp.zeros((9, 2, 128), jnp.bfloat16)
        return carry

    lax.fori_loop(0, owners // 8, clear, 0)

    def body(g, carry):
        base = pl.multiple_of(g * 16, 16)
        w = weight_ref[pl.ds(base, 16), :]
        left = left_ref[pl.ds(base, 16)].astype(jnp.float32) * w[:, None, :]
        left = left.astype(jnp.bfloat16).reshape(512, 128)
        right = right_ref[pl.ds(base, 16)].reshape(512, 128)
        tiles = []
        for part in range(4):
            c = lax.dot_general(
                left[part * 128 : part * 128 + 128],
                right[part * 128 : part * 128 + 128],
                (((1,), (1,)), ((), ())),
                preferred_element_type=jnp.float32,
            )
            for t in range(4):
                rows = [c[32 * t + 8 * k : 32 * t + 8 * k + 8, :] for k in range(4)]
                rows = [
                    rows[k] if k == t else pltpu.roll(rows[k], (32 * (k - t)) % 128, 1)
                    for k in range(4)
                ]
                tiles.append(pick(rows, group).reshape(4, 2, 128).astype(jnp.bfloat16))
        for t, tile in enumerate(tiles):
            owner = owner_ref[base + t]
            slot = count_ref[owner]
            count_ref[owner] = slot + 1
            tag_ref[owner * 2 + slot] = block_ref[base + t]
            out_ref[owner, pl.ds(slot * 4, 4)] = tile
        return carry

    lax.fori_loop(0, left_ref.shape[0] // 16, body, 0)

    def label(o, carry):
        for u in range(8):
            tags = [tag_ref[o * 16 + 2 * u + slot] for slot in range(2)]
            high = jnp.where(sub == 0, tags[0] >> 4, tags[1] >> 4)
            low = jnp.where(sub == 0, tags[0] & 15, tags[1] & 15)
            tile = jnp.where(lane == 0, high, low).astype(jnp.float32)
            out_ref[o * 8 + u, 8] = tile.astype(jnp.bfloat16)
        return carry

    lax.fori_loop(0, owners // 8, label, 0)


def read_labels(slot_ref, vector_ref, label_ref):
    pairs = slot_ref[slot_ref.shape[0] - 1].astype(jnp.float32)
    labels = jnp.minimum(pairs * 16.0 + pltpu.roll(pairs, 127, 1), 512.0)
    vector_ref[...] = labels.astype(jnp.int32)
    pltpu.sync_copy(vector_ref, label_ref)


def clear(even_ref, odd_ref):
    even_ref[...] = jnp.zeros_like(even_ref)
    odd_ref[...] = jnp.zeros_like(odd_ref)


def add_slots(even_ref, odd_ref, label_ref, slot_ref):
    def add(s, carry):
        for u in range(4):
            at = s * 8 + 2 * u
            place = (s % 8) * 16 + 4 * u
            n, m = label_ref[s // 8, place], label_ref[s // 8, place + 2]
            even_ref[n] = even_ref[n] + slot_ref[at].astype(jnp.float32)
            odd_ref[m] = odd_ref[m] + slot_ref[at + 1].astype(jnp.float32)
        return carry

    lax.fori_loop(0, slot_ref.shape[0] // 8, add, 0)


def spread(blocks, group):
    rows = []
    for t in range(4):
        turned = [
            blocks[j] if j == t else pltpu.roll(blocks[j], (32 * (j - t)) % 128, 1) for j in range(4)
        ]
        rows.append(pick(turned, group))
    return rows


def where_am_i():
    ylo, x, z, core, yhi = (lax.axis_index(a) for a in AXES)
    return ylo * 4 + x, z * 2 + core, yhi


def collect_kernel(
    mask_ref, slot_ref, core_ref, base_ref, pattern_ref, even_ref, odd_ref, vector_ref, label_ref
):
    clear(even_ref, odd_ref)
    read_labels(slot_ref, vector_ref, label_ref)
    add_slots(even_ref, odd_ref, label_ref, slot_ref)
    row, col, half_own = where_am_i()
    group = lanes_group((8, 128))

    def body(i, carry):
        r0 = pl.multiple_of(i * 32, 32)
        for side in range(2):
            half = half_own if side == 0 else 1 - half_own
            for jt in range(2):
                j0 = half * 8 + jt * 4
                n = i * 16 + j0
                blocks = [even_ref[n + j] + odd_ref[n + j] for j in range(4)]
                marks = []
                for j in range(4):
                    on = (mask_ref[i, j0 + j] != 0) | (row * 32 + i == col * 16 + j0 + j)
                    marks.append(jnp.full((8, 128), jnp.where(on, 1.0, 0.0)))
                pat = pick(marks, group)
                c0 = pl.multiple_of(half * 256 + jt * 128, 128)
                at = slice(side * 256 + jt * 128, side * 256 + jt * 128 + 128)
                base_ref[pl.ds(r0, 32), at] = core_ref[pl.ds(r0, 32), pl.ds(c0, 128)] + (
                    jnp.concatenate(spread(blocks, group), axis=0)
                )
                pattern_ref[pl.ds(r0, 32), at] = jnp.concatenate([pat] * 4, axis=0).astype(jnp.bfloat16)
        return carry

    lax.fori_loop(0, 32, body, 0)


def assemble_kernel(
    far_ref, base_ref, pattern_ref, ks_ref, own_ref, panel_ref,
    even_ref, odd_ref, vector_ref, label_ref, slot_ref, sem, *, scale,
):
    step = pl.program_id(0)

    @pl.when(step == 0)
    def _():
        load = pltpu.make_async_copy(far_ref, slot_ref, sem)
        load.start()
        clear(even_ref, odd_ref)
        load.wait()
        read_labels(slot_ref, vector_ref, label_ref)
        add_slots(even_ref, odd_ref, label_ref, slot_ref)

    row, col, half_own = where_am_i()
    apart = step ^ (2 * (col & 1) + half_own)
    kept = jnp.where(apart == 0, 0, jnp.where(apart == 2, 1, 2))
    group = lanes_group((8, 128))
    slant = lax.broadcasted_iota(jnp.int32, (32, 128), 0) - lax.broadcasted_iota(jnp.int32, (32, 128), 1)

    def body(i, carry):
        r0 = pl.multiple_of(i * 32, 32)
        for side in range(2):
            half = half_own if side == 0 else 1 - half_own
            for jt in range(2):
                n = step * 128 + i * 16 + half * 8 + jt * 4
                blocks = [even_ref[n + j] + odd_ref[n + j] for j in range(4)]
                at = slice(side * 256 + jt * 128, side * 256 + jt * 128 + 128)
                ks = base_ref[pl.ds(r0, 32), at] + jnp.concatenate(spread(blocks, group), axis=0)
                gap = col * 512 + half * 256 + jt * 128 - row * 1024 - step * 256 - r0
                identity = jnp.where(slant == gap, 0.5, 0.0)
                pat = pattern_ref[pl.ds(r0, 32), at].astype(jnp.float32)
                x = (pat * (identity - scale * ks)).astype(jnp.bfloat16)
                panel_ref[kept, pl.ds(r0, 32), at] = x
                if side == 0:
                    ks_ref[pl.ds(r0, 32), at] = ks
                    own_ref[pl.ds(r0, 32), at] = x
        return carry

    lax.fori_loop(0, 8, body, 0, unroll=4)


VMEM = pl.BlockSpec(memory_space=pltpu.VMEM)
SMEM = pl.BlockSpec(memory_space=pltpu.SMEM)


def contribute(owner, block, left, right, weight):
    tasks = left.shape[0]
    return pl.pallas_call(
        contribute_kernel,
        out_shape=jax.ShapeDtypeStruct((tasks, 9, 2, 128), jnp.bfloat16),
        in_specs=[SMEM, SMEM, VMEM, VMEM, VMEM],
        out_specs=VMEM,
        scratch_shapes=[pltpu.SMEM((tasks,), jnp.int32), pltpu.SMEM((2 * tasks,), jnp.int32)],
        compiler_params=pltpu.CompilerParams(vmem_limit_bytes=12 * 2**20),
        name="contribute",
    )(owner, block, left, right, weight)


ADDERS = [
    pltpu.VMEM((520, 8, 128), jnp.float32),
    pltpu.VMEM((520, 8, 128), jnp.float32),
    pltpu.VMEM((8, 128), jnp.int32),
    pltpu.SMEM((8, 128), jnp.int32),
]


def collect(mask, slots, core):
    return pl.pallas_call(
        collect_kernel,
        out_shape=(
            jax.ShapeDtypeStruct((1024, 512), jnp.float32),
            jax.ShapeDtypeStruct((1024, 512), jnp.bfloat16),
        ),
        in_specs=[SMEM, VMEM, VMEM],
        out_specs=(VMEM, VMEM),
        scratch_shapes=ADDERS,
        cost_estimate=pl.CostEstimate(flops=1 << 20, bytes_accessed=1 << 23, transcendentals=0),
        compiler_params=pltpu.CompilerParams(vmem_limit_bytes=20 * 2**20),
        name="collect",
    )(mask, slots, core)


def assemble(slots, base, pattern):
    def quarter(i):
        return (i, 0)

    return pl.pallas_call(
        functools.partial(assemble_kernel, scale=COUPLING / math.sqrt(NBLK * BS)),
        out_shape=(
            jax.ShapeDtypeStruct((1024, 256), jnp.float32),
            jax.ShapeDtypeStruct((1024, 256), jnp.bfloat16),
            jax.ShapeDtypeStruct((3, 256, 512), jnp.bfloat16),
        ),
        grid=(4,),
        in_specs=[
            pl.BlockSpec(memory_space=pl.ANY),
            pl.BlockSpec((256, 512), quarter),
            pl.BlockSpec((256, 512), quarter),
        ],
        out_specs=(
            pl.BlockSpec((256, 256), quarter),
            pl.BlockSpec((256, 256), quarter),
            pl.BlockSpec((3, 256, 512), lambda i: (0, 0, 0)),
        ),
        scratch_shapes=ADDERS + [pltpu.VMEM((257, 8, 128), jnp.bfloat16), pltpu.SemaphoreType.DMA],
        compiler_params=pltpu.CompilerParams(vmem_limit_bytes=20 * 2**20),
        name="assemble",
    )(slots, base, pattern)


def ring_of(n, step):
    return [(i, (i + step) % n) for i in range(n)]


def gather_z(own, last_up):
    pieces = [own]
    up = down = own
    for s in range(1, 5):
        if s < 4 or last_up:
            up = lax.ppermute(up, "z", ring_of(8, 1))
            pieces.append(up)
        if s < 4 or not last_up:
            down = lax.ppermute(down, "z", ring_of(8, -1))
            pieces.append(down)
    return jnp.stack(pieces)


def place_in_ring(distance):
    distance = distance & 7
    return jnp.where(distance >= 4, 15 - 2 * distance, 2 * distance)


def gather_rows(unit, ylo, x, z):
    fwd, bwd = ring_of(4, 1), ring_of(4, -1)
    near = lax.ppermute(unit, "ylo", SWAP)
    a1 = lax.ppermute(unit, "x", fwd)
    a3 = lax.ppermute(unit, "x", bwd)
    b1, a2 = lax.ppermute(jnp.stack([near, a1]), "x", fwd)
    b3 = lax.ppermute(near, "x", bwd)
    b2 = lax.ppermute(b3, "x", bwd)
    out = jnp.zeros((8,) + unit.shape, unit.dtype)
    for flip, dx, piece in (
        (0, 0, unit), (1, 0, near), (0, 3, a1), (0, 1, a3),
        (1, 3, b1), (1, 1, b3), (0, 2, a2), (1, 2, b2),
    ):
        source = (ylo ^ flip) * 4 + ((x + dx) & 3)
        out = lax.dynamic_update_index_in_dim(out, piece, place_in_ring(source - z), 0)
    return out


def dot(a, b):
    return jnp.einsum("dmk,dkn->mn", a, b, preferred_element_type=jnp.float32)


def product(a, b, chunks):
    far = lax.ppermute(dot(a, b[:, :, 512:]).astype(jnp.bfloat16), "core", SWAP)
    near = lax.optimization_barrier(dot(a, b[:, :, :512]))
    step = a.shape[1] // chunks
    out = []
    for m in range(chunks):
        rows = slice(step * m, step * m + step)
        part = near[rows, 256:] + far[rows, 256:].astype(jnp.float32)
        part = part.astype(jnp.bfloat16)
        if m > 0:
            part, _ = lax.optimization_barrier((part, out[-1][2]))
        away = lax.ppermute(part, "yhi", SWAP)
        out.append((near[rows, :256], far[rows, :256], away))
    return out


def local(basis_left, basis_right, grid_weight, task_owner, task_block, core_matrix, block_mask):
    ylo, x, z = (lax.axis_index(a) for a in AXES[:3])
    tasks = basis_left.shape[0]

    outgoing = contribute(task_owner[:, 0], task_block, basis_left, basis_right, grid_weight)
    arrived = lax.all_to_all(
        outgoing, AXES[:4], split_axis=0, concat_axis=0, tiled=True
    )
    slots = arrived[:, :8].reshape(2 * tasks, 8, 128)
    tag = arrived[:, 8, :, :2]
    tag_tile = jnp.pad(tag.reshape(4, 128), ((0, 4), (0, 0)))[None]
    slots = jnp.concatenate([slots, tag_tile], axis=0)
    far = lax.ppermute(slots, "yhi", SWAP)

    base, pattern = collect(block_mask, slots, core_matrix)
    ks_out, own, panel = assemble(far, base, pattern)

    keep, give = panel[0], lax.ppermute(panel[1], "core", SWAP)
    unit = jnp.concatenate([keep, give], axis=1)
    b = gather_rows(unit, ylo, x, z)
    squares = []
    for m, (near, far, away) in enumerate(product(gather_z(own, True), b, 2)):
        if m > 0:
            away, _ = lax.optimization_barrier((away, squares[0]))
        mask = pattern[512 * m : 512 * m + 512, :256].astype(jnp.float32)
        squares.append(mask * (near + far.astype(jnp.float32) + away.astype(jnp.float32)))
    a2 = [gather_z(square.astype(jnp.bfloat16), m == 0) for m, square in enumerate(squares)]
    ((near, far, away),) = product(jnp.concatenate(a2, axis=1), b, 1)
    cube_term = pattern[:, :256].astype(jnp.float32) * (near + far.astype(jnp.float32) + away.astype(jnp.float32))
    return (ks_out, 3.0 * jnp.concatenate(squares, axis=0) - 2.0 * cube_term)


def solution(mesh):
    fine = Mesh(mesh.devices.reshape(2, 4, 8, 2, 2), AXES)
    spread = AXES
    rows, cols = ("ylo", "x"), ("z", "core")
    placed = (
        P(spread, None, None),
        P(spread, None, None),
        P(spread, None),
        P(spread, None),
        P(spread),
        P(rows, cols),
        P(rows, cols),
    )
    return jax.shard_map(
        local,
        mesh=fine,
        in_specs=placed,
        out_specs=(P(rows, cols + ("yhi",)), P(rows, cols + ("yhi",))),
        check_vma=False,
    )
```

```python
import functools
import math

import jax
import jax.numpy as jnp
from jax import lax
from jax.experimental import pallas as pl
from jax.experimental.pallas import tpu as pltpu
from jax.sharding import Mesh
from jax.sharding import PartitionSpec as P

BS = 32
NBLK = 256
COUPLING = 2.5
AXES = ("ylo", "x", "z", "core", "yhi")
SWAP = [(0, 1), (1, 0)]


def lanes_group(shape):
    return lax.broadcasted_iota(jnp.int32, shape, 1) // BS


def pick(pieces, group):
    out = pieces[0]
    for k in range(1, 4):
        out = jnp.where(group == k, pieces[k], out)
    return out


def contribute_kernel(owner_ref, block_ref, left_ref, right_ref, weight_ref, out_ref, count_ref, tag_ref):
    owners = count_ref.shape[0]
    group = lanes_group((8, 128))
    sub = lax.broadcasted_iota(jnp.int32, (2, 128), 0)
    lane = lax.broadcasted_iota(jnp.int32, (2, 128), 1)

    def clear(o, carry):
        for u in range(8):
            count_ref[o * 8 + u] = 0
            tag_ref[o * 16 + 2 * u] = 512
            tag_ref[o * 16 + 2 * u + 1] = 512
            out_ref[o * 8 + u] = jnp.zeros((9, 2, 128), jnp.bfloat16)
        return carry

    lax.fori_loop(0, owners // 8, clear, 0)

    def body(g, carry):
        base = pl.multiple_of(g * 16, 16)
        w = weight_ref[pl.ds(base, 16), :]
        left = left_ref[pl.ds(base, 16)].astype(jnp.float32) * w[:, None, :]
        left = left.astype(jnp.bfloat16).reshape(512, 128)
        right = right_ref[pl.ds(base, 16)].reshape(512, 128)
        tiles = []
        for part in range(4):
            c = lax.dot_general(
                left[part * 128 : part * 128 + 128],
                right[part * 128 : part * 128 + 128],
                (((1,), (1,)), ((), ())),
                preferred_element_type=jnp.float32,
            )
            for t in range(4):
                rows = [c[32 * t + 8 * k : 32 * t + 8 * k + 8, :] for k in range(4)]
                rows = [
                    rows[k] if k == t else pltpu.roll(rows[k], (32 * (k - t)) % 128, 1)
                    for k in range(4)
                ]
                tiles.append(pick(rows, group).reshape(4, 2, 128).astype(jnp.bfloat16))
        for t, tile in enumerate(tiles):
            owner = owner_ref[base + t]
            slot = count_ref[owner]
            count_ref[owner] = slot + 1
            tag_ref[owner * 2 + slot] = block_ref[base + t]
            out_ref[owner, pl.ds(slot * 4, 4)] = tile
        return carry

    lax.fori_loop(0, left_ref.shape[0] // 16, body, 0)

    def label(o, carry):
        for u in range(8):
            tags = [tag_ref[o * 16 + 2 * u + slot] for slot in range(2)]
            high = jnp.where(sub == 0, tags[0] >> 4, tags[1] >> 4)
            low = jnp.where(sub == 0, tags[0] & 15, tags[1] & 15)
            tile = jnp.where(lane == 0, high, low).astype(jnp.float32)
            out_ref[o * 8 + u, 8] = tile.astype(jnp.bfloat16)
        return carry

    lax.fori_loop(0, owners // 8, label, 0)


def read_labels(slot_ref, vector_ref, label_ref):
    pairs = slot_ref[slot_ref.shape[0] - 1].astype(jnp.float32)
    labels = jnp.minimum(pairs * 16.0 + pltpu.roll(pairs, 127, 1), 512.0)
    vector_ref[...] = labels.astype(jnp.int32)
    pltpu.sync_copy(vector_ref, label_ref)


def clear(even_ref, odd_ref):
    even_ref[...] = jnp.zeros_like(even_ref)
    odd_ref[...] = jnp.zeros_like(odd_ref)


def add_slots(even_ref, odd_ref, label_ref, slot_ref):
    def add(s, carry):
        for u in range(4):
            at = s * 8 + 2 * u
            place = (s % 8) * 16 + 4 * u
            n, m = label_ref[s // 8, place], label_ref[s // 8, place + 2]
            even_ref[n] = even_ref[n] + slot_ref[at].astype(jnp.float32)
            odd_ref[m] = odd_ref[m] + slot_ref[at + 1].astype(jnp.float32)
        return carry

    lax.fori_loop(0, slot_ref.shape[0] // 8, add, 0)


def spread(blocks, group):
    rows = []
    for t in range(4):
        turned = [
            blocks[j] if j == t else pltpu.roll(blocks[j], (32 * (j - t)) % 128, 1) for j in range(4)
        ]
        rows.append(pick(turned, group))
    return rows


def where_am_i():
    ylo, x, z, core, yhi = (lax.axis_index(a) for a in AXES)
    return ylo * 4 + x, z * 2 + core, yhi


def collect_kernel(
    mask_ref, slot_ref, core_ref, base_ref, pattern_ref, even_ref, odd_ref, vector_ref, label_ref
):
    clear(even_ref, odd_ref)
    read_labels(slot_ref, vector_ref, label_ref)
    add_slots(even_ref, odd_ref, label_ref, slot_ref)
    row, col, half_own = where_am_i()
    group = lanes_group((8, 128))

    def body(i, carry):
        r0 = pl.multiple_of(i * 32, 32)
        for side in range(2):
            half = half_own if side == 0 else 1 - half_own
            for jt in range(2):
                j0 = half * 8 + jt * 4
                n = i * 16 + j0
                blocks = [even_ref[n + j] + odd_ref[n + j] for j in range(4)]
                marks = []
                for j in range(4):
                    on = (mask_ref[i, j0 + j] != 0) | (row * 32 + i == col * 16 + j0 + j)
                    marks.append(jnp.full((8, 128), jnp.where(on, 1.0, 0.0)))
                pat = pick(marks, group)
                c0 = pl.multiple_of(half * 256 + jt * 128, 128)
                at = slice(side * 256 + jt * 128, side * 256 + jt * 128 + 128)
                base_ref[pl.ds(r0, 32), at] = core_ref[pl.ds(r0, 32), pl.ds(c0, 128)] + (
                    jnp.concatenate(spread(blocks, group), axis=0)
                )
                pattern_ref[pl.ds(r0, 32), at] = jnp.concatenate([pat] * 4, axis=0).astype(jnp.bfloat16)
        return carry

    lax.fori_loop(0, 32, body, 0)


def assemble_kernel(
    far_ref, base_ref, pattern_ref, ks_ref, own_ref, panel_ref,
    even_ref, odd_ref, vector_ref, label_ref, slot_ref, sem, *, scale,
):
    step = pl.program_id(0)

    @pl.when(step == 0)
    def _():
        load = pltpu.make_async_copy(far_ref, slot_ref, sem)
        load.start()
        clear(even_ref, odd_ref)
        load.wait()
        read_labels(slot_ref, vector_ref, label_ref)
        add_slots(even_ref, odd_ref, label_ref, slot_ref)

    row, col, half_own = where_am_i()
    apart = step ^ (2 * (col & 1) + half_own)
    kept = jnp.where(apart == 0, 0, jnp.where(apart == 2, 1, 2))
    group = lanes_group((8, 128))
    slant = lax.broadcasted_iota(jnp.int32, (32, 128), 0) - lax.broadcasted_iota(jnp.int32, (32, 128), 1)

    def body(i, carry):
        r0 = pl.multiple_of(i * 32, 32)
        for side in range(2):
            half = half_own if side == 0 else 1 - half_own
            for jt in range(2):
                n = step * 128 + i * 16 + half * 8 + jt * 4
                blocks = [even_ref[n + j] + odd_ref[n + j] for j in range(4)]
                at = slice(side * 256 + jt * 128, side * 256 + jt * 128 + 128)
                ks = base_ref[pl.ds(r0, 32), at] + jnp.concatenate(spread(blocks, group), axis=0)
                gap = col * 512 + half * 256 + jt * 128 - row * 1024 - step * 256 - r0
                identity = jnp.where(slant == gap, 0.5, 0.0)
                pat = pattern_ref[pl.ds(r0, 32), at].astype(jnp.float32)
                x = (pat * (identity - scale * ks)).astype(jnp.bfloat16)
                panel_ref[kept, pl.ds(r0, 32), at] = x
                if side == 0:
                    ks_ref[pl.ds(r0, 32), at] = ks
                    own_ref[pl.ds(r0, 32), at] = x
        return carry

    lax.fori_loop(0, 8, body, 0, unroll=4)


VMEM = pl.BlockSpec(memory_space=pltpu.VMEM)
SMEM = pl.BlockSpec(memory_space=pltpu.SMEM)


def contribute(owner, block, left, right, weight):
    tasks = left.shape[0]
    return pl.pallas_call(
        contribute_kernel,
        out_shape=jax.ShapeDtypeStruct((tasks, 9, 2, 128), jnp.bfloat16),
        in_specs=[SMEM, SMEM, VMEM, VMEM, VMEM],
        out_specs=VMEM,
        scratch_shapes=[pltpu.SMEM((tasks,), jnp.int32), pltpu.SMEM((2 * tasks,), jnp.int32)],
        name="contribute",
    )(owner, block, left, right, weight)


ADDERS = [
    pltpu.VMEM((520, 8, 128), jnp.float32),
    pltpu.VMEM((520, 8, 128), jnp.float32),
    pltpu.VMEM((8, 128), jnp.int32),
    pltpu.SMEM((8, 128), jnp.int32),
]


def collect(mask, slots, core):
    return pl.pallas_call(
        collect_kernel,
        out_shape=(
            jax.ShapeDtypeStruct((1024, 512), jnp.float32),
            jax.ShapeDtypeStruct((1024, 512), jnp.bfloat16),
        ),
        in_specs=[SMEM, VMEM, VMEM],
        out_specs=(VMEM, VMEM),
        scratch_shapes=ADDERS,
        cost_estimate=pl.CostEstimate(flops=1 << 20, bytes_accessed=1 << 23, transcendentals=0),
        compiler_params=pltpu.CompilerParams(vmem_limit_bytes=20 * 2**20),
        name="collect",
    )(mask, slots, core)


def assemble(slots, base, pattern):
    def quarter(i):
        return (i, 0)

    return pl.pallas_call(
        functools.partial(assemble_kernel, scale=COUPLING / math.sqrt(NBLK * BS)),
        out_shape=(
            jax.ShapeDtypeStruct((1024, 256), jnp.float32),
            jax.ShapeDtypeStruct((1024, 256), jnp.bfloat16),
            jax.ShapeDtypeStruct((3, 256, 512), jnp.bfloat16),
        ),
        grid=(4,),
        in_specs=[
            pl.BlockSpec(memory_space=pl.ANY),
            pl.BlockSpec((256, 512), quarter),
            pl.BlockSpec((256, 512), quarter),
        ],
        out_specs=(
            pl.BlockSpec((256, 256), quarter),
            pl.BlockSpec((256, 256), quarter),
            pl.BlockSpec((3, 256, 512), lambda i: (0, 0, 0)),
        ),
        scratch_shapes=ADDERS + [pltpu.VMEM((257, 8, 128), jnp.bfloat16), pltpu.SemaphoreType.DMA],
        compiler_params=pltpu.CompilerParams(vmem_limit_bytes=20 * 2**20),
        name="assemble",
    )(slots, base, pattern)


def ring_of(n, step):
    return [(i, (i + step) % n) for i in range(n)]


def gather_z(own, last_up):
    pieces = [own]
    up = down = own
    for s in range(1, 5):
        if s < 4 or last_up:
            up = lax.ppermute(up, "z", ring_of(8, 1))
            pieces.append(up)
        if s < 4 or not last_up:
            down = lax.ppermute(down, "z", ring_of(8, -1))
            pieces.append(down)
    return jnp.stack(pieces)


def place_in_ring(distance):
    distance = distance & 7
    return jnp.where(distance >= 4, 15 - 2 * distance, 2 * distance)


def gather_rows(unit, ylo, x, z):
    fwd, bwd = ring_of(4, 1), ring_of(4, -1)
    near = lax.ppermute(unit, "ylo", SWAP)
    a1 = lax.ppermute(unit, "x", fwd)
    a3 = lax.ppermute(unit, "x", bwd)
    b1, a2 = lax.ppermute(jnp.stack([near, a1]), "x", fwd)
    b3 = lax.ppermute(near, "x", bwd)
    b2 = lax.ppermute(b3, "x", bwd)
    out = jnp.zeros((8,) + unit.shape, unit.dtype)
    for flip, dx, piece in (
        (0, 0, unit), (1, 0, near), (0, 3, a1), (0, 1, a3),
        (1, 3, b1), (1, 1, b3), (0, 2, a2), (1, 2, b2),
    ):
        source = (ylo ^ flip) * 4 + ((x + dx) & 3)
        out = lax.dynamic_update_index_in_dim(out, piece, place_in_ring(source - z), 0)
    return out


def dot(a, b):
    return jnp.einsum("dmk,dkn->mn", a, b, preferred_element_type=jnp.float32)


def product(a, b, chunks):
    far = lax.ppermute(dot(a, b[:, :, 512:]).astype(jnp.bfloat16), "core", SWAP)
    near = lax.optimization_barrier(dot(a, b[:, :, :512]))
    step = a.shape[1] // chunks
    out = []
    for m in range(chunks):
        rows = slice(step * m, step * m + step)
        part = near[rows, 256:] + far[rows, 256:].astype(jnp.float32)
        part = part.astype(jnp.bfloat16)
        if m > 0:
            part, _ = lax.optimization_barrier((part, out[-1][2]))
        away = lax.ppermute(part, "yhi", SWAP)
        out.append((near[rows, :256], far[rows, :256], away))
    return out


def local(basis_left, basis_right, grid_weight, task_owner, task_block, core_matrix, block_mask):
    ylo, x, z = (lax.axis_index(a) for a in AXES[:3])
    tasks = basis_left.shape[0]

    outgoing = contribute(task_owner[:, 0], task_block, basis_left, basis_right, grid_weight)
    arrived = lax.all_to_all(
        outgoing, AXES[:4], split_axis=0, concat_axis=0, tiled=True
    )
    slots = arrived[:, :8].reshape(2 * tasks, 8, 128)
    tag = arrived[:, 8, :, :2]
    tag_tile = jnp.pad(tag.reshape(4, 128), ((0, 4), (0, 0)))[None]
    slots = jnp.concatenate([slots, tag_tile], axis=0)
    far = lax.ppermute(slots, "yhi", SWAP)

    base, pattern = collect(block_mask, slots, core_matrix)
    ks_out, own, panel = assemble(far, base, pattern)

    keep, give = panel[0], lax.ppermute(panel[1], "core", SWAP)
    unit = jnp.concatenate([keep, give], axis=1)
    b = gather_rows(unit, ylo, x, z)
    squares = []
    for m, (near, far, away) in enumerate(product(gather_z(own, True), b, 2)):
        if m > 0:
            away, _ = lax.optimization_barrier((away, squares[0]))
        mask = pattern[512 * m : 512 * m + 512, :256].astype(jnp.float32)
        squares.append(mask * (near + far.astype(jnp.float32) + away.astype(jnp.float32)))
    a2 = [gather_z(square.astype(jnp.bfloat16), m == 0) for m, square in enumerate(squares)]
    ((near, far, away),) = product(jnp.concatenate(a2, axis=1), b, 1)
    cube_term = pattern[:, :256].astype(jnp.float32) * (near + far.astype(jnp.float32) + away.astype(jnp.float32))
    return (ks_out, 3.0 * jnp.concatenate(squares, axis=0) - 2.0 * cube_term)


def solution(mesh):
    fine = Mesh(mesh.devices.reshape(2, 4, 8, 2, 2), AXES)
    spread = AXES
    rows, cols = ("ylo", "x"), ("z", "core")
    placed = (
        P(spread, None, None),
        P(spread, None, None),
        P(spread, None),
        P(spread, None),
        P(spread),
        P(rows, cols),
        P(rows, cols),
    )
    return jax.shard_map(
        local,
        mesh=fine,
        in_specs=placed,
        out_specs=(P(rows, cols + ("yhi",)), P(rows, cols + ("yhi",))),
        check_vma=False,
    )
```

```python
import functools
import math

import jax
import jax.numpy as jnp
from jax import lax
from jax.experimental import pallas as pl
from jax.experimental.pallas import tpu as pltpu
from jax.sharding import Mesh
from jax.sharding import PartitionSpec as P

BS = 32
NBLK = 256
COUPLING = 2.5
AXES = ("ylo", "x", "z", "core", "yhi")
SWAP = [(0, 1), (1, 0)]


def lanes_group(shape):
    return lax.broadcasted_iota(jnp.int32, shape, 1) // BS


def pick(pieces, group):
    out = pieces[0]
    for k in range(1, 4):
        out = jnp.where(group == k, pieces[k], out)
    return out


def contribute_kernel(owner_ref, block_ref, left_ref, right_ref, weight_ref, out_ref, count_ref, tag_ref):
    owners = count_ref.shape[0]
    group = lanes_group((8, 128))
    sub = lax.broadcasted_iota(jnp.int32, (2, 128), 0)
    lane = lax.broadcasted_iota(jnp.int32, (2, 128), 1)

    def clear(o, carry):
        for u in range(8):
            count_ref[o * 8 + u] = 0
            tag_ref[o * 16 + 2 * u] = 512
            tag_ref[o * 16 + 2 * u + 1] = 512
            out_ref[o * 8 + u] = jnp.zeros((9, 2, 128), jnp.bfloat16)
        return carry

    step = pl.program_id(0)
    tasks = left_ref.shape[0]

    @pl.when(step == 0)
    def _():
        lax.fori_loop(0, owners // 8, clear, 0)

    def body(g, carry):
        base = pl.multiple_of(g * 16, 16)
        w = weight_ref[pl.ds(base, 16), :]
        left = left_ref[pl.ds(base, 16)].astype(jnp.float32) * w[:, None, :]
        left = left.astype(jnp.bfloat16).reshape(512, 128)
        right = right_ref[pl.ds(base, 16)].reshape(512, 128)
        tiles = []
        for part in range(4):
            c = lax.dot_general(
                left[part * 128 : part * 128 + 128],
                right[part * 128 : part * 128 + 128],
                (((1,), (1,)), ((), ())),
                preferred_element_type=jnp.float32,
            )
            for t in range(4):
                rows = [c[32 * t + 8 * k : 32 * t + 8 * k + 8, :] for k in range(4)]
                rows = [
                    rows[k] if k == t else pltpu.roll(rows[k], (32 * (k - t)) % 128, 1)
                    for k in range(4)
                ]
                tiles.append(pick(rows, group).reshape(4, 2, 128).astype(jnp.bfloat16))
        for t, tile in enumerate(tiles):
            task = step * tasks + base + t
            owner = owner_ref[task]
            slot = count_ref[owner]
            count_ref[owner] = slot + 1
            tag_ref[owner * 2 + slot] = block_ref[task]
            out_ref[owner, pl.ds(slot * 4, 4)] = tile
        return carry

    lax.fori_loop(0, tasks // 16, body, 0)

    def label(o, carry):
        for u in range(8):
            tags = [tag_ref[o * 16 + 2 * u + slot] for slot in range(2)]
            high = jnp.where(sub == 0, tags[0] >> 4, tags[1] >> 4)
            low = jnp.where(sub == 0, tags[0] & 15, tags[1] & 15)
            tile = jnp.where(lane == 0, high, low).astype(jnp.float32)
            out_ref[o * 8 + u, 8] = tile.astype(jnp.bfloat16)
        return carry

    @pl.when(step == pl.num_programs(0) - 1)
    def _():
        lax.fori_loop(0, owners // 8, label, 0)


def read_labels(slot_ref, vector_ref, label_ref):
    pairs = slot_ref[slot_ref.shape[0] - 1].astype(jnp.float32)
    labels = jnp.minimum(pairs * 16.0 + pltpu.roll(pairs, 127, 1), 512.0)
    vector_ref[...] = labels.astype(jnp.int32)
    pltpu.sync_copy(vector_ref, label_ref)


def clear(even_ref, odd_ref):
    even_ref[...] = jnp.zeros_like(even_ref)
    odd_ref[...] = jnp.zeros_like(odd_ref)


def add_slots(even_ref, odd_ref, label_ref, slot_ref):
    def add(s, carry):
        for u in range(4):
            at = s * 8 + 2 * u
            place = (s % 8) * 16 + 4 * u
            n, m = label_ref[s // 8, place], label_ref[s // 8, place + 2]
            even_ref[n] = even_ref[n] + slot_ref[at].astype(jnp.float32)
            odd_ref[m] = odd_ref[m] + slot_ref[at + 1].astype(jnp.float32)
        return carry

    lax.fori_loop(0, slot_ref.shape[0] // 8, add, 0)


def spread(blocks, group):
    rows = []
    for t in range(4):
        turned = [
            blocks[j] if j == t else pltpu.roll(blocks[j], (32 * (j - t)) % 128, 1) for j in range(4)
        ]
        rows.append(pick(turned, group))
    return rows


def where_am_i():
    ylo, x, z, core, yhi = (lax.axis_index(a) for a in AXES)
    return ylo * 4 + x, z * 2 + core, yhi


def collect_kernel(
    mask_ref, slot_ref, core_ref, base_ref, pattern_ref, even_ref, odd_ref, vector_ref, label_ref
):
    clear(even_ref, odd_ref)
    read_labels(slot_ref, vector_ref, label_ref)
    add_slots(even_ref, odd_ref, label_ref, slot_ref)
    row, col, half_own = where_am_i()
    group = lanes_group((8, 128))

    def body(i, carry):
        r0 = pl.multiple_of(i * 32, 32)
        for side in range(2):
            half = half_own if side == 0 else 1 - half_own
            for jt in range(2):
                j0 = half * 8 + jt * 4
                n = i * 16 + j0
                blocks = [even_ref[n + j] + odd_ref[n + j] for j in range(4)]
                marks = []
                for j in range(4):
                    on = (mask_ref[i, j0 + j] != 0) | (row * 32 + i == col * 16 + j0 + j)
                    marks.append(jnp.full((8, 128), jnp.where(on, 1.0, 0.0)))
                pat = pick(marks, group)
                c0 = pl.multiple_of(half * 256 + jt * 128, 128)
                at = slice(side * 256 + jt * 128, side * 256 + jt * 128 + 128)
                base_ref[pl.ds(r0, 32), at] = core_ref[pl.ds(r0, 32), pl.ds(c0, 128)] + (
                    jnp.concatenate(spread(blocks, group), axis=0)
                )
                pattern_ref[pl.ds(r0, 32), at] = jnp.concatenate([pat] * 4, axis=0).astype(jnp.bfloat16)
        return carry

    lax.fori_loop(0, 32, body, 0)


def assemble_kernel(
    far_ref, base_ref, pattern_ref, ks_ref, own_ref, panel_ref,
    even_ref, odd_ref, vector_ref, label_ref, slot_ref, sem, *, scale,
):
    step = pl.program_id(0)

    @pl.when(step == 0)
    def _():
        load = pltpu.make_async_copy(far_ref, slot_ref, sem)
        load.start()
        clear(even_ref, odd_ref)
        load.wait()
        read_labels(slot_ref, vector_ref, label_ref)
        add_slots(even_ref, odd_ref, label_ref, slot_ref)

    row, col, half_own = where_am_i()
    apart = step ^ (2 * (col & 1) + half_own)
    kept = jnp.where(apart == 0, 0, jnp.where(apart == 2, 1, 2))
    group = lanes_group((8, 128))
    slant = lax.broadcasted_iota(jnp.int32, (32, 128), 0) - lax.broadcasted_iota(jnp.int32, (32, 128), 1)

    def body(i, carry):
        r0 = pl.multiple_of(i * 32, 32)
        for side in range(2):
            half = half_own if side == 0 else 1 - half_own
            for jt in range(2):
                n = step * 128 + i * 16 + half * 8 + jt * 4
                blocks = [even_ref[n + j] + odd_ref[n + j] for j in range(4)]
                at = slice(side * 256 + jt * 128, side * 256 + jt * 128 + 128)
                ks = base_ref[pl.ds(r0, 32), at] + jnp.concatenate(spread(blocks, group), axis=0)
                gap = col * 512 + half * 256 + jt * 128 - row * 1024 - step * 256 - r0
                identity = jnp.where(slant == gap, 0.5, 0.0)
                pat = pattern_ref[pl.ds(r0, 32), at].astype(jnp.float32)
                x = (pat * (identity - scale * ks)).astype(jnp.bfloat16)
                panel_ref[kept, pl.ds(r0, 32), at] = x
                if side == 0:
                    ks_ref[pl.ds(r0, 32), at] = ks
                    own_ref[pl.ds(r0, 32), at] = x
        return carry

    lax.fori_loop(0, 8, body, 0, unroll=4)


VMEM = pl.BlockSpec(memory_space=pltpu.VMEM)
SMEM = pl.BlockSpec(memory_space=pltpu.SMEM)


def contribute(owner, block, left, right, weight):
    tasks = left.shape[0]
    return pl.pallas_call(
        contribute_kernel,
        out_shape=jax.ShapeDtypeStruct((tasks, 9, 2, 128), jnp.bfloat16),
        grid=(2,),
        in_specs=[
            SMEM,
            SMEM,
            pl.BlockSpec((tasks // 2, 32, 128), lambda i: (i, 0, 0)),
            pl.BlockSpec((tasks // 2, 32, 128), lambda i: (i, 0, 0)),
            pl.BlockSpec((tasks // 2, 128), lambda i: (i, 0)),
        ],
        out_specs=pl.BlockSpec((tasks, 9, 2, 128), lambda i: (0, 0, 0, 0)),
        scratch_shapes=[pltpu.SMEM((tasks,), jnp.int32), pltpu.SMEM((2 * tasks,), jnp.int32)],
        name="contribute",
    )(owner, block, left, right, weight)


ADDERS = [
    pltpu.VMEM((520, 8, 128), jnp.float32),
    pltpu.VMEM((520, 8, 128), jnp.float32),
    pltpu.VMEM((8, 128), jnp.int32),
    pltpu.SMEM((8, 128), jnp.int32),
]


def collect(mask, slots, core):
    return pl.pallas_call(
        collect_kernel,
        out_shape=(
            jax.ShapeDtypeStruct((1024, 512), jnp.float32),
            jax.ShapeDtypeStruct((1024, 512), jnp.bfloat16),
        ),
        in_specs=[SMEM, VMEM, VMEM],
        out_specs=(VMEM, VMEM),
        scratch_shapes=ADDERS,
        cost_estimate=pl.CostEstimate(flops=1 << 20, bytes_accessed=1 << 23, transcendentals=0),
        compiler_params=pltpu.CompilerParams(vmem_limit_bytes=20 * 2**20),
        name="collect",
    )(mask, slots, core)


def assemble(slots, base, pattern):
    def quarter(i):
        return (i, 0)

    return pl.pallas_call(
        functools.partial(assemble_kernel, scale=COUPLING / math.sqrt(NBLK * BS)),
        out_shape=(
            jax.ShapeDtypeStruct((1024, 256), jnp.float32),
            jax.ShapeDtypeStruct((1024, 256), jnp.bfloat16),
            jax.ShapeDtypeStruct((3, 256, 512), jnp.bfloat16),
        ),
        grid=(4,),
        in_specs=[
            pl.BlockSpec(memory_space=pl.ANY),
            pl.BlockSpec((256, 512), quarter),
            pl.BlockSpec((256, 512), quarter),
        ],
        out_specs=(
            pl.BlockSpec((256, 256), quarter),
            pl.BlockSpec((256, 256), quarter),
            pl.BlockSpec((3, 256, 512), lambda i: (0, 0, 0)),
        ),
        scratch_shapes=ADDERS + [pltpu.VMEM((257, 8, 128), jnp.bfloat16), pltpu.SemaphoreType.DMA],
        compiler_params=pltpu.CompilerParams(vmem_limit_bytes=20 * 2**20),
        name="assemble",
    )(slots, base, pattern)


def ring_of(n, step):
    return [(i, (i + step) % n) for i in range(n)]


def gather_z(own, last_up):
    pieces = [own]
    up = down = own
    for s in range(1, 5):
        if s < 4 or last_up:
            up = lax.ppermute(up, "z", ring_of(8, 1))
            pieces.append(up)
        if s < 4 or not last_up:
            down = lax.ppermute(down, "z", ring_of(8, -1))
            pieces.append(down)
    return jnp.stack(pieces)


def place_in_ring(distance):
    distance = distance & 7
    return jnp.where(distance >= 4, 15 - 2 * distance, 2 * distance)


def gather_rows(unit, ylo, x, z):
    fwd, bwd = ring_of(4, 1), ring_of(4, -1)
    near = lax.ppermute(unit, "ylo", SWAP)
    a1 = lax.ppermute(unit, "x", fwd)
    a3 = lax.ppermute(unit, "x", bwd)
    b1, a2 = lax.ppermute(jnp.stack([near, a1]), "x", fwd)
    b3 = lax.ppermute(near, "x", bwd)
    b2 = lax.ppermute(b3, "x", bwd)
    out = jnp.zeros((8,) + unit.shape, unit.dtype)
    for flip, dx, piece in (
        (0, 0, unit), (1, 0, near), (0, 3, a1), (0, 1, a3),
        (1, 3, b1), (1, 1, b3), (0, 2, a2), (1, 2, b2),
    ):
        source = (ylo ^ flip) * 4 + ((x + dx) & 3)
        out = lax.dynamic_update_index_in_dim(out, piece, place_in_ring(source - z), 0)
    return out


def dot(a, b):
    return jnp.einsum("dmk,dkn->mn", a, b, preferred_element_type=jnp.float32)


def product(a, b, chunks):
    far = lax.ppermute(dot(a, b[:, :, 512:]).astype(jnp.bfloat16), "core", SWAP)
    near = lax.optimization_barrier(dot(a, b[:, :, :512]))
    step = a.shape[1] // chunks
    out = []
    for m in range(chunks):
        rows = slice(step * m, step * m + step)
        part = near[rows, 256:] + far[rows, 256:].astype(jnp.float32)
        part = part.astype(jnp.bfloat16)
        if m > 0:
            part, _ = lax.optimization_barrier((part, out[-1][2]))
        away = lax.ppermute(part, "yhi", SWAP)
        out.append((near[rows, :256], far[rows, :256], away))
    return out


def local(basis_left, basis_right, grid_weight, task_owner, task_block, core_matrix, block_mask):
    ylo, x, z = (lax.axis_index(a) for a in AXES[:3])
    tasks = basis_left.shape[0]

    outgoing = contribute(task_owner[:, 0], task_block, basis_left, basis_right, grid_weight)
    arrived = lax.all_to_all(
        outgoing, AXES[:4], split_axis=0, concat_axis=0, tiled=True
    )
    slots = arrived[:, :8].reshape(2 * tasks, 8, 128)
    tag = arrived[:, 8, :, :2]
    tag_tile = jnp.pad(tag.reshape(4, 128), ((0, 4), (0, 0)))[None]
    slots = jnp.concatenate([slots, tag_tile], axis=0)
    far = lax.ppermute(slots, "yhi", SWAP)

    base, pattern = collect(block_mask, slots, core_matrix)
    ks_out, own, panel = assemble(far, base, pattern)

    keep, give = panel[0], lax.ppermute(panel[1], "core", SWAP)
    unit = jnp.concatenate([keep, give], axis=1)
    b = gather_rows(unit, ylo, x, z)
    squares = []
    for m, (near, far, away) in enumerate(product(gather_z(own, True), b, 2)):
        if m > 0:
            away, _ = lax.optimization_barrier((away, squares[0]))
        mask = pattern[512 * m : 512 * m + 512, :256].astype(jnp.float32)
        squares.append(mask * (near + far.astype(jnp.float32) + away.astype(jnp.float32)))
    a2 = [gather_z(square.astype(jnp.bfloat16), m == 0) for m, square in enumerate(squares)]
    ((near, far, away),) = product(jnp.concatenate(a2, axis=1), b, 1)
    cube_term = pattern[:, :256].astype(jnp.float32) * (near + far.astype(jnp.float32) + away.astype(jnp.float32))
    return (ks_out, 3.0 * jnp.concatenate(squares, axis=0) - 2.0 * cube_term)


def solution(mesh):
    fine = Mesh(mesh.devices.reshape(2, 4, 8, 2, 2), AXES)
    spread = AXES
    rows, cols = ("ylo", "x"), ("z", "core")
    placed = (
        P(spread, None, None),
        P(spread, None, None),
        P(spread, None),
        P(spread, None),
        P(spread),
        P(rows, cols),
        P(rows, cols),
    )
    return jax.shard_map(
        local,
        mesh=fine,
        in_specs=placed,
        out_specs=(P(rows, cols + ("yhi",)), P(rows, cols + ("yhi",))),
        check_vma=False,
    )
```

```python
import functools
import math

import jax
import jax.numpy as jnp
from jax import lax
from jax.experimental import pallas as pl
from jax.experimental.pallas import tpu as pltpu
from jax.sharding import Mesh
from jax.sharding import PartitionSpec as P

BS = 32
NBLK = 256
COUPLING = 2.5
AXES = ("ylo", "x", "z", "core", "yhi")
SWAP = [(0, 1), (1, 0)]


def lanes_group(shape):
    return lax.broadcasted_iota(jnp.int32, shape, 1) // BS


def pick(pieces, group):
    out = pieces[0]
    for k in range(1, 4):
        out = jnp.where(group == k, pieces[k], out)
    return out


def contribute_kernel(owner_ref, block_ref, left_ref, right_ref, weight_ref, out_ref, count_ref, tag_ref):
    owners = count_ref.shape[0]
    group = lanes_group((8, 128))
    sub = lax.broadcasted_iota(jnp.int32, (2, 128), 0)
    lane = lax.broadcasted_iota(jnp.int32, (2, 128), 1)

    def clear(o, carry):
        for u in range(8):
            count_ref[o * 8 + u] = 0
            tag_ref[o * 16 + 2 * u] = 512
            tag_ref[o * 16 + 2 * u + 1] = 512
            out_ref[o * 8 + u] = jnp.zeros((9, 2, 128), jnp.bfloat16)
        return carry

    step = pl.program_id(0)
    tasks = left_ref.shape[0]

    @pl.when(step == 0)
    def _():
        lax.fori_loop(0, owners // 8, clear, 0)

    def body(g, carry):
        base = pl.multiple_of(g * 16, 16)
        w = weight_ref[pl.ds(base, 16), :]
        left = left_ref[pl.ds(base, 16)].astype(jnp.float32) * w[:, None, :]
        left = left.astype(jnp.bfloat16).reshape(512, 128)
        right = right_ref[pl.ds(base, 16)].reshape(512, 128)
        tiles = []
        for part in range(4):
            c = lax.dot_general(
                left[part * 128 : part * 128 + 128],
                right[part * 128 : part * 128 + 128],
                (((1,), (1,)), ((), ())),
                preferred_element_type=jnp.float32,
            )
            for t in range(4):
                rows = [c[32 * t + 8 * k : 32 * t + 8 * k + 8, :] for k in range(4)]
                rows = [
                    rows[k] if k == t else pltpu.roll(rows[k], (32 * (k - t)) % 128, 1)
                    for k in range(4)
                ]
                tiles.append(pick(rows, group).reshape(4, 2, 128).astype(jnp.bfloat16))
        for t, tile in enumerate(tiles):
            task = step * tasks + base + t
            owner = owner_ref[task]
            slot = count_ref[owner]
            count_ref[owner] = slot + 1
            tag_ref[owner * 2 + slot] = block_ref[task]
            out_ref[owner, pl.ds(slot * 4, 4)] = tile
        return carry

    lax.fori_loop(0, tasks // 16, body, 0)

    def label(o, carry):
        for u in range(8):
            tags = [tag_ref[o * 16 + 2 * u + slot] for slot in range(2)]
            high = jnp.where(sub == 0, tags[0] >> 4, tags[1] >> 4)
            low = jnp.where(sub == 0, tags[0] & 15, tags[1] & 15)
            tile = jnp.where(lane == 0, high, low).astype(jnp.float32)
            out_ref[o * 8 + u, 8] = tile.astype(jnp.bfloat16)
        return carry

    @pl.when(step == pl.num_programs(0) - 1)
    def _():
        lax.fori_loop(0, owners // 8, label, 0)


def read_labels(slot_ref, vector_ref, label_ref):
    pairs = slot_ref[slot_ref.shape[0] - 1].astype(jnp.float32)
    labels = jnp.minimum(pairs * 16.0 + pltpu.roll(pairs, 127, 1), 512.0)
    vector_ref[...] = labels.astype(jnp.int32)
    pltpu.sync_copy(vector_ref, label_ref)


def clear(even_ref, odd_ref):
    even_ref[...] = jnp.zeros_like(even_ref)
    odd_ref[...] = jnp.zeros_like(odd_ref)


def add_slots(even_ref, odd_ref, label_ref, slot_ref):
    def add(s, carry):
        for u in range(4):
            at = s * 8 + 2 * u
            place = (s % 8) * 16 + 4 * u
            n, m = label_ref[s // 8, place], label_ref[s // 8, place + 2]
            even_ref[n] = even_ref[n] + slot_ref[at].astype(jnp.float32)
            odd_ref[m] = odd_ref[m] + slot_ref[at + 1].astype(jnp.float32)
        return carry

    lax.fori_loop(0, slot_ref.shape[0] // 8, add, 0)


def spread(blocks, group):
    rows = []
    for t in range(4):
        turned = [
            blocks[j] if j == t else pltpu.roll(blocks[j], (32 * (j - t)) % 128, 1) for j in range(4)
        ]
        rows.append(pick(turned, group))
    return rows


def where_am_i():
    ylo, x, z, core, yhi = (lax.axis_index(a) for a in AXES)
    return ylo * 4 + x, z * 2 + core, yhi


def collect_kernel(
    mask_ref, slot_ref, core_ref, base_ref, pattern_ref, even_ref, odd_ref, vector_ref, label_ref
):
    clear(even_ref, odd_ref)
    read_labels(slot_ref, vector_ref, label_ref)
    add_slots(even_ref, odd_ref, label_ref, slot_ref)
    row, col, half_own = where_am_i()
    group = lanes_group((8, 128))

    def body(i, carry):
        r0 = pl.multiple_of(i * 32, 32)
        for side in range(2):
            half = half_own if side == 0 else 1 - half_own
            for jt in range(2):
                j0 = half * 8 + jt * 4
                n = i * 16 + j0
                blocks = [even_ref[n + j] + odd_ref[n + j] for j in range(4)]
                marks = []
                for j in range(4):
                    on = (mask_ref[i, j0 + j] != 0) | (row * 32 + i == col * 16 + j0 + j)
                    marks.append(jnp.full((8, 128), jnp.where(on, 1.0, 0.0)))
                pat = pick(marks, group)
                c0 = pl.multiple_of(half * 256 + jt * 128, 128)
                at = slice(side * 256 + jt * 128, side * 256 + jt * 128 + 128)
                base_ref[pl.ds(r0, 32), at] = core_ref[pl.ds(r0, 32), pl.ds(c0, 128)] + (
                    jnp.concatenate(spread(blocks, group), axis=0)
                )
                pattern_ref[pl.ds(r0, 32), at] = jnp.concatenate([pat] * 4, axis=0).astype(jnp.bfloat16)
        return carry

    lax.fori_loop(0, 32, body, 0)


def assemble_kernel(
    far_ref, base_ref, pattern_ref, ks_ref, own_ref, panel_ref,
    even_ref, odd_ref, vector_ref, label_ref, slot_ref, sem, *, scale,
):
    step = pl.program_id(0)

    @pl.when(step == 0)
    def _():
        load = pltpu.make_async_copy(far_ref, slot_ref, sem)
        load.start()
        clear(even_ref, odd_ref)
        load.wait()
        read_labels(slot_ref, vector_ref, label_ref)
        add_slots(even_ref, odd_ref, label_ref, slot_ref)

    row, col, half_own = where_am_i()
    apart = step ^ (2 * (col & 1) + half_own)
    kept = jnp.where(apart == 0, 0, jnp.where(apart == 2, 1, 2))
    group = lanes_group((8, 128))
    slant = lax.broadcasted_iota(jnp.int32, (32, 128), 0) - lax.broadcasted_iota(jnp.int32, (32, 128), 1)

    def body(i, carry):
        r0 = pl.multiple_of(i * 32, 32)
        for side in range(2):
            half = half_own if side == 0 else 1 - half_own
            for jt in range(2):
                n = step * 128 + i * 16 + half * 8 + jt * 4
                blocks = [even_ref[n + j] + odd_ref[n + j] for j in range(4)]
                at = slice(side * 256 + jt * 128, side * 256 + jt * 128 + 128)
                ks = base_ref[pl.ds(r0, 32), at] + jnp.concatenate(spread(blocks, group), axis=0)
                gap = col * 512 + half * 256 + jt * 128 - row * 1024 - step * 256 - r0
                identity = jnp.where(slant == gap, 0.5, 0.0)
                pat = pattern_ref[pl.ds(r0, 32), at].astype(jnp.float32)
                x = (pat * (identity - scale * ks)).astype(jnp.bfloat16)
                panel_ref[kept, pl.ds(r0, 32), at] = x
                if side == 0:
                    ks_ref[pl.ds(r0, 32), at] = ks
                    own_ref[pl.ds(r0, 32), at] = x
        return carry

    lax.fori_loop(0, 8, body, 0, unroll=4)


VMEM = pl.BlockSpec(memory_space=pltpu.VMEM)
SMEM = pl.BlockSpec(memory_space=pltpu.SMEM)


def contribute(owner, block, left, right, weight):
    tasks = left.shape[0]
    return pl.pallas_call(
        contribute_kernel,
        out_shape=jax.ShapeDtypeStruct((tasks, 9, 2, 128), jnp.bfloat16),
        grid=(4,),
        in_specs=[
            SMEM,
            SMEM,
            pl.BlockSpec((tasks // 4, 32, 128), lambda i: (i, 0, 0)),
            pl.BlockSpec((tasks // 4, 32, 128), lambda i: (i, 0, 0)),
            pl.BlockSpec((tasks // 4, 128), lambda i: (i, 0)),
        ],
        out_specs=pl.BlockSpec((tasks, 9, 2, 128), lambda i: (0, 0, 0, 0)),
        scratch_shapes=[pltpu.SMEM((tasks,), jnp.int32), pltpu.SMEM((2 * tasks,), jnp.int32)],
        name="contribute",
    )(owner, block, left, right, weight)


ADDERS = [
    pltpu.VMEM((520, 8, 128), jnp.float32),
    pltpu.VMEM((520, 8, 128), jnp.float32),
    pltpu.VMEM((8, 128), jnp.int32),
    pltpu.SMEM((8, 128), jnp.int32),
]


def collect(mask, slots, core):
    return pl.pallas_call(
        collect_kernel,
        out_shape=(
            jax.ShapeDtypeStruct((1024, 512), jnp.float32),
            jax.ShapeDtypeStruct((1024, 512), jnp.bfloat16),
        ),
        in_specs=[SMEM, VMEM, VMEM],
        out_specs=(VMEM, VMEM),
        scratch_shapes=ADDERS,
        cost_estimate=pl.CostEstimate(flops=1 << 20, bytes_accessed=1 << 23, transcendentals=0),
        compiler_params=pltpu.CompilerParams(vmem_limit_bytes=20 * 2**20),
        name="collect",
    )(mask, slots, core)


def assemble(slots, base, pattern):
    def quarter(i):
        return (i, 0)

    return pl.pallas_call(
        functools.partial(assemble_kernel, scale=COUPLING / math.sqrt(NBLK * BS)),
        out_shape=(
            jax.ShapeDtypeStruct((1024, 256), jnp.float32),
            jax.ShapeDtypeStruct((1024, 256), jnp.bfloat16),
            jax.ShapeDtypeStruct((3, 256, 512), jnp.bfloat16),
        ),
        grid=(4,),
        in_specs=[
            pl.BlockSpec(memory_space=pl.ANY),
            pl.BlockSpec((256, 512), quarter),
            pl.BlockSpec((256, 512), quarter),
        ],
        out_specs=(
            pl.BlockSpec((256, 256), quarter),
            pl.BlockSpec((256, 256), quarter),
            pl.BlockSpec((3, 256, 512), lambda i: (0, 0, 0)),
        ),
        scratch_shapes=ADDERS + [pltpu.VMEM((257, 8, 128), jnp.bfloat16), pltpu.SemaphoreType.DMA],
        compiler_params=pltpu.CompilerParams(vmem_limit_bytes=20 * 2**20),
        name="assemble",
    )(slots, base, pattern)


def ring_of(n, step):
    return [(i, (i + step) % n) for i in range(n)]


def gather_z(own, last_up):
    pieces = [own]
    up = down = own
    for s in range(1, 5):
        if s < 4 or last_up:
            up = lax.ppermute(up, "z", ring_of(8, 1))
            pieces.append(up)
        if s < 4 or not last_up:
            down = lax.ppermute(down, "z", ring_of(8, -1))
            pieces.append(down)
    return jnp.stack(pieces)


def place_in_ring(distance):
    distance = distance & 7
    return jnp.where(distance >= 4, 15 - 2 * distance, 2 * distance)


def gather_rows(unit, ylo, x, z):
    fwd, bwd = ring_of(4, 1), ring_of(4, -1)
    near = lax.ppermute(unit, "ylo", SWAP)
    a1 = lax.ppermute(unit, "x", fwd)
    a3 = lax.ppermute(unit, "x", bwd)
    b1, a2 = lax.ppermute(jnp.stack([near, a1]), "x", fwd)
    b3 = lax.ppermute(near, "x", bwd)
    b2 = lax.ppermute(b3, "x", bwd)
    out = jnp.zeros((8,) + unit.shape, unit.dtype)
    for flip, dx, piece in (
        (0, 0, unit), (1, 0, near), (0, 3, a1), (0, 1, a3),
        (1, 3, b1), (1, 1, b3), (0, 2, a2), (1, 2, b2),
    ):
        source = (ylo ^ flip) * 4 + ((x + dx) & 3)
        out = lax.dynamic_update_index_in_dim(out, piece, place_in_ring(source - z), 0)
    return out


def dot(a, b):
    return jnp.einsum("dmk,dkn->mn", a, b, preferred_element_type=jnp.float32)


def product(a, b, chunks):
    far = lax.ppermute(dot(a, b[:, :, 512:]).astype(jnp.bfloat16), "core", SWAP)
    near = lax.optimization_barrier(dot(a, b[:, :, :512]))
    step = a.shape[1] // chunks
    out = []
    for m in range(chunks):
        rows = slice(step * m, step * m + step)
        part = near[rows, 256:] + far[rows, 256:].astype(jnp.float32)
        part = part.astype(jnp.bfloat16)
        if m > 0:
            part, _ = lax.optimization_barrier((part, out[-1][2]))
        away = lax.ppermute(part, "yhi", SWAP)
        out.append((near[rows, :256], far[rows, :256], away))
    return out


def local(basis_left, basis_right, grid_weight, task_owner, task_block, core_matrix, block_mask):
    ylo, x, z = (lax.axis_index(a) for a in AXES[:3])
    tasks = basis_left.shape[0]

    outgoing = contribute(task_owner[:, 0], task_block, basis_left, basis_right, grid_weight)
    arrived = lax.all_to_all(
        outgoing, AXES[:4], split_axis=0, concat_axis=0, tiled=True
    )
    slots = arrived[:, :8].reshape(2 * tasks, 8, 128)
    tag = arrived[:, 8, :, :2]
    tag_tile = jnp.pad(tag.reshape(4, 128), ((0, 4), (0, 0)))[None]
    slots = jnp.concatenate([slots, tag_tile], axis=0)
    far = lax.ppermute(slots, "yhi", SWAP)

    base, pattern = collect(block_mask, slots, core_matrix)
    ks_out, own, panel = assemble(far, base, pattern)

    keep, give = panel[0], lax.ppermute(panel[1], "core", SWAP)
    unit = jnp.concatenate([keep, give], axis=1)
    b = gather_rows(unit, ylo, x, z)
    squares = []
    for m, (near, far, away) in enumerate(product(gather_z(own, True), b, 2)):
        if m > 0:
            away, _ = lax.optimization_barrier((away, squares[0]))
        mask = pattern[512 * m : 512 * m + 512, :256].astype(jnp.float32)
        squares.append(mask * (near + far.astype(jnp.float32) + away.astype(jnp.float32)))
    a2 = [gather_z(square.astype(jnp.bfloat16), m == 0) for m, square in enumerate(squares)]
    ((near, far, away),) = product(jnp.concatenate(a2, axis=1), b, 1)
    cube_term = pattern[:, :256].astype(jnp.float32) * (near + far.astype(jnp.float32) + away.astype(jnp.float32))
    return (ks_out, 3.0 * jnp.concatenate(squares, axis=0) - 2.0 * cube_term)


def solution(mesh):
    fine = Mesh(mesh.devices.reshape(2, 4, 8, 2, 2), AXES)
    spread = AXES
    rows, cols = ("ylo", "x"), ("z", "core")
    placed = (
        P(spread, None, None),
        P(spread, None, None),
        P(spread, None),
        P(spread, None),
        P(spread),
        P(rows, cols),
        P(rows, cols),
    )
    return jax.shard_map(
        local,
        mesh=fine,
        in_specs=placed,
        out_specs=(P(rows, cols + ("yhi",)), P(rows, cols + ("yhi",))),
        check_vma=False,
    )
```
